128 devices in a mesh: mode: 16 (over z_hi, y, core), gx: 2 (over z_lo), gy: 4 (over x).
Axes of the slice: x: 4, y: 4, z: 4 (z_hi: 2, z_lo: 2; z = z_hi * 2 + z_lo), core: 2. Of those that a mesh axis runs over, the one named last changes fastest.
Arguments:
- right_side: float32 [16, 32, 28672], P('gx', 'gy', 'mode'), may hold values from -6 to 6
- col_block: int32 [224, 32], P('mode'), may hold values from 0 to 223, as said below
- blocks: bfloat16 [224, 32, 128, 128], P('mode'), may hold values from -0.09375 to 0.09375
- relax_rate: float32 [28672], P('mode'), may hold values from 0.5 to 4
- drift_speed: float32 [2, 28672], P(None, 'mode'), may hold values from 0.3 to 1.5
- upwind_sign: int32 [2, 28672], P(None, 'mode'), may hold values from 0 to 1
- wall_mask: int32 [16, 32], P('gx', 'gy'), may hold values 0 or 1
Outputs:
- solution: float32 [16, 32, 28672], P('gx', 'gy', 'mode')
- hessenberg: float32 [4, 3], replicated
The draws below stay inside these ranges and needn't reach their ends.
Inputs may be any that keep to these rules, and one draw needn't show every extreme that they name: `col_block`: for every block row and every o in 0 .. 15, slots o * 2 to (o + 1) * 2 - 1 hold distinct column blocks of o * 14 to (o + 1) * 14 - 1.
All inputs are finite; a program needn't handle non-finite values. No bound on the sum of `wall_mask` on one device may be relied on, other than what follows from the above.
Results may differ from the reference program's by a relative error of at most 0.00081.
Values may be sent and summed in bfloat16 or wider, within the bound.
A program may use at most 128 MiB of HBM per device.

```python
import math
import jax
import jax.numpy as jnp
from jax import lax

BLOCK = 128
MB_DEV = 14
PER_OWNER = 2
KRYLOV = 3
MODE_BLOCKS = 224
MODES = 28672
NNZ = 32
NX = 16
NY = 32


def draw_col_block(key, part):
    owners = MODE_BLOCKS // MB_DEV
    scores = jax.random.randint(key, (MODE_BLOCKS, owners, MB_DEV), 0, 1 << 20)
    scores = scores * MB_DEV + jnp.arange(MB_DEV, dtype=jnp.int32)
    order = jnp.argsort(scores, axis=-1, stable=True)[:, :, :PER_OWNER]
    shifted = order + (jnp.arange(owners, dtype=jnp.int32) * MB_DEV)[None, :, None]
    return shifted.reshape(MODE_BLOCKS, owners * PER_OWNER).astype(jnp.int32)


def place_ends(values, key, smallest, largest):
    dims = values.shape
    spot = [jax.random.randint(jax.random.fold_in(key, axis), (), 0, dims[axis]) for axis in range(len(dims))]
    values = values.at[tuple(spot)].set(smallest)
    longest = dims.index(max(dims))
    spot[longest] = (spot[longest] + 1) % dims[longest]
    return values.at[tuple(spot)].set(largest)


def shard_levels(own_key, shape, cuts, low, high):
    def one(axis_at, parts):
        steps = jax.random.uniform(jax.random.fold_in(jax.random.fold_in(own_key, 6), axis_at), (parts,), jnp.float32, low / len(cuts), high / len(cuts))
        return jnp.repeat(jnp.exp(steps), shape[axis_at] // parts).reshape((-1,) + (1,) * (len(shape) - axis_at - 1))

    loudness = one(*cuts[0])
    for cut in cuts[1:]:
        loudness = loudness * one(*cut)
    return loudness


def scatter_about(stream_key, shape, deviation, most, pieces=(), kind=jnp.bfloat16):
    gain = shard_levels(stream_key, shape, pieces, -0.22, 0.18) if pieces else 1.0
    result = jax.random.normal(stream_key, shape, jnp.float32) * deviation * gain
    return jnp.minimum(jnp.maximum(result, -most), most).astype(kind)


def setup_inputs(seed: int = 0) -> dict:
    key_of = jax.random.split(jax.random.key(seed), 8)
    return {
        "right_side": scatter_about(key_of[0], (NX, NY, MODES), 1.0, 6.0, ((0, 2), (1, 4), (2, 16)), jnp.float32),
        "col_block": draw_col_block(jax.random.fold_in(key_of[7], 71), 0),
        "blocks": scatter_about(key_of[2], (MODE_BLOCKS, NNZ, BLOCK, BLOCK), (NNZ * BLOCK) ** -0.5, 0.09375, ((0, 16),)),
        "relax_rate": jnp.clip(jnp.exp(math.log(4.0) - 2.0794415 * jax.random.uniform(key_of[3], (MODES,), jnp.float32) ** shard_levels(key_of[3], (MODES,), ((0, 16),), -0.2, 0.2)), 0.5, 4.0),
        "drift_speed": jnp.clip(jnp.exp(math.log(1.5) - 1.60943787 * jax.random.uniform(key_of[4], (2, MODES), jnp.float32) ** shard_levels(key_of[4], (2, MODES), ((1, 16),), -0.2, 0.2)), 0.3, 1.5),
        "upwind_sign": place_ends(jax.random.randint(key_of[5], (2, MODES), 0, 2), jax.random.fold_in(key_of[5], 1), 0, 1).astype(jnp.int32),
        "wall_mask": place_ends((jax.random.randint(key_of[6], (NX, NY), 0, 8) < 1).astype(jnp.int32), jax.random.fold_in(key_of[6], 1), 0, 1),
    }


epsilon = 1e-12

def apply_operator(current, col_block, blocks, relax_rate, drift_speed, upwind_sign, open_cells):
    masked = current * open_cells[:, :, None]
    padded = jnp.pad(masked, ((1, 1), (1, 1), (0, 0)))
    from_west = padded[:-2, 1:-1]
    from_east = padded[2:, 1:-1]
    from_south = padded[1:-1, :-2]
    from_north = padded[1:-1, 2:]
    upstream_first = jnp.where(upwind_sign[0] == 1, from_west, from_east)
    upstream_second = jnp.where(upwind_sign[1] == 1, from_south, from_north)
    drift_term = drift_speed[0] * (current - upstream_first) + drift_speed[1] * (current - upstream_second)
    rounded = current.astype(jnp.bfloat16).reshape(NX * NY, MODE_BLOCKS, BLOCK)

    def block_row(pair):
        columns, weights = pair
        picked = jnp.take(rounded, columns, axis=1).astype(jnp.float32)
        return jnp.einsum('sik,csk->ci', weights.astype(jnp.float32), picked, precision=lax.Precision.HIGHEST)
    scattered = lax.map(block_row, (col_block, blocks))
    scattered = jnp.transpose(scattered, (1, 0, 2)).reshape(NX, NY, MODES)
    return relax_rate * current + drift_term - scattered

def least_squares(hessenberg, initial):
    upper = [[hessenberg[row_index, col_index] for col_index in range(KRYLOV)] for row_index in range(KRYLOV + 1)]
    target = [initial] + [jnp.zeros_like(initial) for row_index in range(KRYLOV)]
    cosines = []
    sines = []
    for col_index in range(KRYLOV):
        for row_index in range(col_index):
            first = upper[row_index][col_index]
            second = upper[row_index + 1][col_index]
            upper[row_index][col_index] = cosines[row_index] * first + sines[row_index] * second
            upper[row_index + 1][col_index] = cosines[row_index] * second - sines[row_index] * first
        first = upper[col_index][col_index]
        second = upper[col_index + 1][col_index]
        radius = jnp.sqrt(first * first + second * second)
        cosine = first / radius
        sine_value = second / radius
        upper[col_index][col_index] = radius
        target[col_index + 1] = -sine_value * target[col_index]
        target[col_index] = cosine * target[col_index]
        cosines.append(cosine)
        sines.append(sine_value)
    combo = [None] * KRYLOV
    for row_index in reversed(range(KRYLOV)):
        running = target[row_index]
        for col_index in range(row_index + 1, KRYLOV):
            running = running - upper[row_index][col_index] * combo[col_index]
        combo[row_index] = running / upper[row_index][row_index]
    return combo

def reference(right_side, col_block, blocks, relax_rate, drift_speed, upwind_sign, wall_mask):
    open_cells = (1 - wall_mask).astype(jnp.float32)
    initial = jnp.sqrt(jnp.sum(right_side * right_side) + epsilon)
    krylov_basis = [right_side / initial]
    columns_list = []
    for section in range(KRYLOV):
        mapped = apply_operator(krylov_basis[section], col_block, blocks, relax_rate, drift_speed, upwind_sign, open_cells)
        coefficients = [jnp.sum(krylov_basis[earlier] * mapped) for earlier in range(section + 1)]
        remainder = mapped
        for earlier in range(section + 1):
            remainder = remainder - coefficients[earlier] * krylov_basis[earlier]
        length = jnp.sqrt(jnp.sum(remainder * remainder) + epsilon)
        krylov_basis.append(remainder / length)
        entries = coefficients + [length] + [jnp.zeros_like(length) for later in range(KRYLOV - section - 1)]
        columns_list.append(jnp.stack(entries))
    hessenberg = jnp.stack(columns_list, axis=1)
    combo = least_squares(hessenberg, initial)
    solution = jnp.zeros_like(right_side)
    for section in range(KRYLOV):
        solution = solution + combo[section] * krylov_basis[section]
    return (solution, hessenberg)
```

```python
import functools

import jax
import jax.numpy as jnp
from jax import lax
from jax.experimental import pallas as pl
from jax.experimental.pallas import tpu as pltpu
from jax.sharding import PartitionSpec as P

KRYLOV = 3
MESH = pl.DeviceIdType.MESH
LANES = 128
ROWS = 16

epsilon = 1e-12

WIRE = ("A1", "A3", "Z0", "A2", "B1", "B3", "Z1", "Z3", "C2")
PLACES = [(dz, dy) for dz in range(2) for dy in range(4)]


def least_squares(upper, initial, zero):
    target = [initial] + [zero for row_index in range(KRYLOV)]
    cosines = []
    sines = []
    for col_index in range(KRYLOV):
        for row_index in range(col_index):
            first = upper[row_index][col_index]
            second = upper[row_index + 1][col_index]
            upper[row_index][col_index] = cosines[row_index] * first + sines[row_index] * second
            upper[row_index + 1][col_index] = cosines[row_index] * second - sines[row_index] * first
        first = upper[col_index][col_index]
        second = upper[col_index + 1][col_index]
        radius = jnp.sqrt(first * first + second * second)
        cosine = first / radius
        sine_value = second / radius
        upper[col_index][col_index] = radius
        target[col_index + 1] = -sine_value * target[col_index]
        target[col_index] = cosine * target[col_index]
        cosines.append(cosine)
        sines.append(sine_value)
    combo = [None] * KRYLOV
    for row_index in reversed(range(KRYLOV)):
        running = target[row_index]
        for col_index in range(row_index + 1, KRYLOV):
            running = running - upper[row_index][col_index] * combo[col_index]
        combo[row_index] = running / upper[row_index][row_index]
    return combo


def gram_schmidt(gram, shift, initial):
    size = KRYLOV + 1

    def inner(first, second):
        total = None
        for i in range(size):
            if first[i] is None:
                continue
            row = None
            for k in range(size):
                if second[k] is None:
                    continue
                term = gram[min(i, k)][max(i, k)] * second[k]
                row = term if row is None else row + term
            term = first[i] * row
            total = term if total is None else total + term
        return total

    one = jnp.ones_like(initial)
    zero = jnp.zeros_like(initial)
    basis = [[one, None, None, None]]
    hessenberg = [[zero for col in range(KRYLOV)] for row in range(size)]
    for section in range(KRYLOV):
        current = basis[section]
        mapped = [None] * size
        for i in range(size):
            if current[i] is not None:
                own = shift * current[i]
                mapped[i] = own if mapped[i] is None else mapped[i] + own
                mapped[i + 1] = current[i]
        coefficients = [inner(basis[i], mapped) for i in range(section + 1)]
        for i in range(section + 1):
            hessenberg[i][section] = coefficients[i]
            for k in range(size):
                if basis[i][k] is not None:
                    mapped[k] = mapped[k] - coefficients[i] * basis[i][k]
        length = jnp.sqrt(jnp.maximum(inner(mapped, mapped), 0.0) + epsilon)
        hessenberg[section + 1][section] = length
        basis.append([None if value is None else value / length for value in mapped])
    combo = least_squares([list(row) for row in hessenberg], initial, zero)
    weights = []
    for k in range(KRYLOV):
        total = None
        for section in range(KRYLOV):
            if basis[section][k] is not None:
                term = combo[section] * basis[section][k]
                total = term if total is None else total + term
        weights.append(total)
    return hessenberg, weights


def kernel(
    col_ref,
    wall_ref,
    right_ref,
    relax_ref,
    drift_ref,
    sign_ref,
    blocks_ref,
    out_ref,
    hess_ref,
    weights,
    base,
    tile_one,
    tile_two,
    gather_one,
    gather_two,
    face_out,
    face_in,
    open_ref,
    w_sem,
    bulk_send,
    bulk_recv,
    pass_send,
    pass_recv,
    face_send,
    face_recv,
    one_send,
    one_recv,
    two_send,
    two_recv,
    *slots,
):
    krylov = slots[: KRYLOV + 1]
    held = [
        {(dz, dy, dc): slots[KRYLOV + 1 + 16 * j + 8 * dc + 4 * dz + dy] for dz, dy in PLACES for dc in range(2)}
        for j in range(KRYLOV)
    ]
    local_blocks = col_ref.shape[0]
    halves = (local_blocks - local_blocks // 2, local_blocks // 2)
    starts = (0, halves[0])

    mode = lax.axis_index("mode")
    gx = lax.axis_index("gx")
    gy = lax.axis_index("gy")
    zh = mode // 8
    y = (mode // 2) % 4
    core = mode % 2

    def mode_of(dz, dy, dc):
        return lax.rem(zh + dz, 2) * 8 + lax.rem(y + dy, 4) * 2 + lax.rem(core + dc, 2)

    def lanes_of(b):
        return pl.ds(pl.multiple_of(b * LANES, LANES), LANES)

    def weight_copies(dz, dy, dc):
        owner = mode_of(dz, dy, dc)
        place = 8 * dc + 4 * dz + dy
        return [
            pltpu.make_async_copy(
                blocks_ref.at[:, owner * 2 + s],
                weights.at[place, :, :, pl.ds(s * LANES, LANES)],
                w_sem.at[place, s],
            )
            for s in range(2)
        ]

    order = [
        (0, 0, 0), (0, 0, 1), (0, 1, 0), (0, 3, 0), (1, 0, 0), (0, 1, 1), (0, 3, 1), (1, 0, 1),
        (0, 2, 0), (0, 2, 1), (1, 1, 0), (1, 3, 0), (1, 1, 1), (1, 3, 1), (1, 2, 0), (1, 2, 1),
    ]
    for place in order:
        for copy in weight_copies(*place):
            copy.start()

    barrier = pltpu.get_barrier_semaphore()
    for d in range(1, 16):
        pl.semaphore_signal(barrier, inc=1, device_id={"mode": lax.rem(mode + d, 16)}, device_id_type=MESH)
    for d in range(1, 8):
        pl.semaphore_signal(
            barrier, inc=1, device_id={"gx": lax.rem(gx + d // 4, 2), "gy": lax.rem(gy + d % 4, 4)}, device_id_type=MESH
        )

    def norm_block(b, carry):
        plain, weighted = carry
        lanes = lanes_of(b)
        diagonal = relax_ref[0:1, lanes] + drift_ref[0:1, lanes] + drift_ref[1:2, lanes]
        for x in range(8):
            value = right_ref[x, :, lanes]
            square = value * value
            plain = plain + square
            weighted = weighted + square * diagonal
        return plain, weighted

    empty = jnp.zeros((8, LANES), jnp.float32)
    plain, weighted = lax.fori_loop(0, local_blocks, norm_block, (empty, empty))
    for x in range(8):
        for cell in range(8):
            open_ref[pl.ds(x * 8 + cell, 1), :] = jnp.full(
                (1, LANES), (1 - wall_ref[x, cell]).astype(jnp.float32), jnp.float32
            )

    pl.semaphore_wait(barrier, 22)

    def summed(which, rows):
        tile = jnp.concatenate(
            [jnp.sum(row, axis=0, keepdims=True) for row in rows]
            + [jnp.zeros((ROWS - len(rows), LANES), jnp.float32)],
            axis=0,
        )
        tile_one[which] = tile
        gather_one[which, mode] = tile
        copies = []
        for d in range(1, 16):
            copies.append(
                pltpu.make_async_remote_copy(
                    src_ref=tile_one.at[which],
                    dst_ref=gather_one.at[which, mode],
                    send_sem=one_send.at[which, d],
                    recv_sem=one_recv.at[which, d],
                    device_id={"mode": lax.rem(mode + d, 16)},
                    device_id_type=MESH,
                )
            )
        for copy in copies:
            copy.start()
        for copy in copies:
            copy.wait()
        total = gather_one[which, 0]
        for source in range(1, 16):
            total = total + gather_one[which, source]
        group = gx * 4 + gy
        tile_two[which] = total
        gather_two[which, group] = total
        copies = []
        for d in range(1, 8):
            copies.append(
                pltpu.make_async_remote_copy(
                    src_ref=tile_two.at[which],
                    dst_ref=gather_two.at[which, group],
                    send_sem=two_send.at[which, d],
                    recv_sem=two_recv.at[which, d],
                    device_id={"gx": lax.rem(gx + d // 4, 2), "gy": lax.rem(gy + d % 4, 4)},
                    device_id_type=MESH,
                )
            )
        for copy in copies:
            copy.start()
        for copy in copies:
            copy.wait()
        total = gather_two[which, 0]
        for source in range(1, 8):
            total = total + gather_two[which, source]
        total = jnp.broadcast_to(jnp.sum(total, axis=1, keepdims=True), (ROWS, LANES))
        tile_one[which] = total
        return [tile_one[which, pl.ds(k, 1), :] for k in range(len(rows))]

    squared, diagonal = summed(0, [plain, weighted])
    initial = jnp.sqrt(squared + epsilon)
    shift = diagonal / (squared + epsilon)

    def first_block(b, carry):
        lanes = lanes_of(b)
        value = (right_ref[:, :, lanes] / initial).reshape(64, LANES)
        krylov[0][b] = value
        held[0][0, 0, 0][b] = value.astype(jnp.bfloat16)
        return carry

    lax.fori_loop(0, local_blocks, first_block, 0)

    sends = []
    rows8 = lax.broadcasted_iota(jnp.int32, (8, LANES), 0)
    grams = {}

    for j in range(KRYLOV):
        x = held[j]
        now = krylov[j]
        later = krylov[j + 1]

        def wire(name, half, source, target, to):
            part = pl.ds(starts[half], halves[half])
            index = WIRE.index(name)
            return pltpu.make_async_remote_copy(
                src_ref=x[source].at[part],
                dst_ref=x[target].at[part],
                send_sem=bulk_send.at[j, index, half],
                recv_sem=bulk_recv.at[j, index, half],
                device_id={"mode": to},
                device_id_type=MESH,
            )

        below, above, across, beside = mode_of(0, 3, 0), mode_of(0, 1, 0), mode_of(1, 0, 0), mode_of(0, 0, 1)
        routes = {
            "A1": ((0, 0, 0), (0, 1, 0), below),
            "A3": ((0, 0, 0), (0, 3, 0), above),
            "Z0": ((0, 0, 0), (1, 0, 0), across),
            "B1": ((1, 0, 0), (1, 1, 0), below),
            "B3": ((1, 0, 0), (1, 3, 0), above),
            "Z1": ((0, 1, 0), (1, 1, 0), across),
            "Z3": ((0, 3, 0), (1, 3, 0), across),
        }

        def copy_of(name, half):
            if name == "A2":
                source, target, to = ((0, 1, 0), (0, 2, 0), below) if half == 0 else ((0, 3, 0), (0, 2, 0), above)
            elif name == "C2":
                source, target, to = ((1, 3, 0), (1, 2, 0), above) if half == 0 else ((1, 1, 0), (1, 2, 0), below)
            else:
                source, target, to = routes[name]
            return wire(name, half, source, target, to)

        def passing(dz, dy, half):
            part = pl.ds(starts[half], halves[half])
            return pltpu.make_async_remote_copy(
                src_ref=x[dz, dy, 0].at[part],
                dst_ref=x[dz, dy, 1].at[part],
                send_sem=pass_send.at[j, 4 * dz + dy, half],
                recv_sem=pass_recv.at[j, 4 * dz + dy, half],
                device_id={"mode": beside},
                device_id_type=MESH,
            )

        def start(copy):
            copy.start()
            sends.append(copy)

        def take(name, half, place, then=()):
            copy_of(name, half).wait_recv()
            for following in then:
                start(copy_of(following, half))
            start(passing(*place, half))

        for half in range(2):
            for name in ("A1", "A3", "Z0"):
                start(copy_of(name, half))
            start(passing(0, 0, half))

        def face_block(b, carry):
            low, high = now[b, 0:8, :] * open_ref[0:8, :], now[b, 56:64, :] * open_ref[56:64, :]
            face_out[j, 0, b] = jnp.where(gx == 0, high, low)
            for cell in range(8):
                value = now[b, 8 * cell : 8 * cell + 8, :] * open_ref[8 * cell : 8 * cell + 8, :]
                face_out[j, 1, b, pl.ds(cell, 1), :] = value[7:8, :]
                face_out[j, 2, b, pl.ds(cell, 1), :] = value[0:1, :]
            return carry

        lax.fori_loop(0, local_blocks, face_block, 0)
        faces = []
        for side, to in (
            (0, {"gx": lax.rem(gx + 1, 2)}),
            (1, {"gy": lax.rem(gy + 1, 4)}),
            (2, {"gy": lax.rem(gy + 3, 4)}),
        ):
            copy = pltpu.make_async_remote_copy(
                src_ref=face_out.at[j, side],
                dst_ref=face_in.at[j, side],
                send_sem=face_send.at[j, side],
                recv_sem=face_recv.at[j, side],
                device_id=to,
                device_id_type=MESH,
            )
            start(copy)
            faces.append(copy)

        def product(place, b):
            owner = mode_of(*place)
            first, second = (
                jnp.clip(col_ref[b, owner * 2 + s] - owner * local_blocks, 0, local_blocks - 1) for s in range(2)
            )
            ref = x[place]
            picked = jnp.concatenate([ref[first], ref[second]], axis=1)
            matrix = weights[8 * place[2] + 4 * place[0] + place[1], b]
            return lax.dot_general(picked, matrix, (((1,), (1,)), ((), ())), preferred_element_type=jnp.float32)

        def ready(place):
            if j == 0:
                for copy in weight_copies(*place):
                    copy.wait()
            if place[2] == 1:
                for half in range(2):
                    passing(place[0], place[1], half).wait_recv()

        def compute(place):
            ready(place)

            def block(b, carry):
                later[b] = later[b] - product(place, b)
                return carry

            lax.fori_loop(0, local_blocks, block, 0)

        def compute_first(place):
            ready(place)

            def block(b, carry):
                later[b] = -product(place, b)
                return carry

            lax.fori_loop(0, local_blocks, block, 0)

        def local_terms():
            for copy in faces:
                copy.wait_recv()

            def block(b, carry):
                lanes = lanes_of(b)
                relax = relax_ref[0:1, lanes] - shift
                speed_first, speed_second = drift_ref[0:1, lanes], drift_ref[1:2, lanes]
                to_higher_first = sign_ref[0:1, lanes] == 1
                to_higher_second = sign_ref[1:2, lanes] == 1
                edge = face_in[j, 0, b]
                values = [now[b, 8 * cell : 8 * cell + 8, :] for cell in range(8)]
                masked = [values[cell] * open_ref[8 * cell : 8 * cell + 8, :] for cell in range(8)]
                west = [jnp.where(gx == 1, edge, 0.0)] + masked[:7]
                east = masked[1:] + [jnp.where(gx == 0, edge, 0.0)]
                for cell in range(8):
                    rows = slice(8 * cell, 8 * cell + 8)
                    from_low = jnp.where(gy > 0, face_in[j, 1, b, pl.ds(cell, 1), :], 0.0)
                    from_high = jnp.where(gy < 3, face_in[j, 2, b, pl.ds(cell, 1), :], 0.0)
                    south = jnp.where(rows8 == 0, from_low, pltpu.roll(masked[cell], 1, 0))
                    north = jnp.where(rows8 == 7, from_high, pltpu.roll(masked[cell], 7, 0))
                    upstream_first = jnp.where(to_higher_first, west[cell], east[cell])
                    upstream_second = jnp.where(to_higher_second, south, north)
                    value = values[cell]
                    term = speed_first * (value - upstream_first) + speed_second * (value - upstream_second)
                    later[b, rows, :] = later[b, rows, :] + (relax * value + term)
                return carry

            lax.fori_loop(0, local_blocks, block, 0)

        def dots_with(k):
            def block(b, carry):
                totals = list(carry)
                for cell in range(8):
                    rows = slice(8 * cell, 8 * cell + 8)
                    value = krylov[k][b, rows, :]
                    for i in range(k + 1):
                        totals[i] = totals[i] + krylov[i][b, rows, :] * value
                return tuple(totals)

            totals = lax.fori_loop(0, local_blocks, block, tuple(empty for i in range(k + 1)))
            for i in range(k + 1):
                grams[i, k] = totals[i]

        compute_first((0, 0, 0))
        take("A1", 0, (0, 1), ("A2", "Z1"))
        take("A3", 0, (0, 3))
        compute((0, 0, 1))
        take("Z0", 0, (1, 0), ("B3",))
        take("A1", 1, (0, 1))
        take("A3", 1, (0, 3), ("A2", "Z3"))
        compute((0, 1, 0))
        compute((0, 3, 0))
        take("Z0", 1, (1, 0), ("B1",))
        compute((1, 0, 0))
        compute((0, 1, 1))
        take("A2", 0, (0, 2))
        take("A2", 1, (0, 2))
        compute((0, 3, 1))
        take("B3", 0, (1, 3), ("C2",))
        compute((1, 0, 1))
        local_terms()
        take("B1", 1, (1, 1), ("C2",))
        compute((0, 2, 0))
        dots_with(j)
        compute((0, 2, 1))
        take("Z1", 0, (1, 1))
        take("Z3", 1, (1, 3))
        compute((1, 1, 0))
        compute((1, 3, 0))
        take("C2", 0, (1, 2))
        take("C2", 1, (1, 2))
        compute((1, 1, 1))
        compute((1, 3, 1))
        compute((1, 2, 0))
        place = (1, 2, 1)
        ready(place)
        if j < KRYLOV - 1:
            nearby = held[j + 1][0, 0, 0]

            def last_block(b, carry):
                value = later[b] - product(place, b)
                later[b] = value
                nearby[b] = value.astype(jnp.bfloat16)
                return carry

            lax.fori_loop(0, local_blocks, last_block, 0)
        else:

            def final_block(b, carry):
                totals = list(carry)
                value = later[b] - product(place, b)
                for cell in range(8):
                    rows = slice(8 * cell, 8 * cell + 8)
                    part = value[rows, :]
                    for i in range(KRYLOV):
                        totals[i] = totals[i] + krylov[i][b, rows, :] * part
                    totals[KRYLOV] = totals[KRYLOV] + part * part
                return tuple(totals)

            totals = lax.fori_loop(0, local_blocks, final_block, tuple(empty for i in range(KRYLOV + 1)))
            for i in range(KRYLOV + 1):
                grams[i, KRYLOV] = totals[i]

    pairs = [(i, k) for k in range(KRYLOV + 1) for i in range(k + 1)]
    sums = dict(zip(pairs, summed(1, [grams[pair] for pair in pairs])))
    gram = [[sums.get((i, k)) for k in range(KRYLOV + 1)] for i in range(KRYLOV + 1)]
    hessenberg, factors = gram_schmidt(gram, shift, initial)

    def out_block(b, carry):
        lanes = lanes_of(b)
        value = factors[0] * krylov[0][b]
        for k in range(1, KRYLOV):
            value = value + factors[k] * krylov[k][b]
        out_ref[:, :, lanes] = value.reshape(8, 8, LANES)
        return carry

    lax.fori_loop(0, local_blocks, out_block, 0)
    columns = lax.broadcasted_iota(jnp.int32, (8, LANES), 1)
    tile = empty
    for i in range(KRYLOV + 1):
        for k in range(KRYLOV):
            tile = jnp.where((rows8 == i) & (columns == k), hessenberg[i][k], tile)
    hess_ref[...] = tile[: KRYLOV + 1, :KRYLOV]
    for copy in sends:
        copy.wait_send()


def per_device(right_side, col_block, blocks, relax_rate, drift_speed, upwind_sign, wall_mask):
    cells_first, cells_second, local_modes = right_side.shape
    cells = cells_first * cells_second
    local_blocks = col_block.shape[0]
    block = blocks.shape[2]
    vector = pltpu.VMEM((local_blocks, cells, block), jnp.float32)
    rounded = pltpu.VMEM((local_blocks, cells, block), jnp.bfloat16)
    dma = pltpu.SemaphoreType.DMA
    vmem = pl.BlockSpec(memory_space=pltpu.VMEM)
    smem = pl.BlockSpec(memory_space=pltpu.SMEM)
    return pl.pallas_call(
        kernel,
        out_shape=(
            jax.ShapeDtypeStruct(right_side.shape, jnp.float32),
            jax.ShapeDtypeStruct((KRYLOV + 1, KRYLOV), jnp.float32),
        ),
        in_specs=[smem, smem, vmem, vmem, vmem, vmem, pl.BlockSpec(memory_space=pl.ANY)],
        out_specs=(vmem, vmem),
        scratch_shapes=[
            pltpu.VMEM((16, local_blocks, block, 2 * block), jnp.bfloat16),
            pltpu.VMEM((8, LANES), jnp.float32),
            pltpu.VMEM((2, ROWS, LANES), jnp.float32),
            pltpu.VMEM((2, ROWS, LANES), jnp.float32),
            pltpu.VMEM((2, 16, ROWS, LANES), jnp.float32),
            pltpu.VMEM((2, 8, ROWS, LANES), jnp.float32),
            pltpu.VMEM((KRYLOV, 3, local_blocks, 8, LANES), jnp.float32),
            pltpu.VMEM((KRYLOV, 3, local_blocks, 8, LANES), jnp.float32),
            pltpu.VMEM((cells, LANES), jnp.float32),
            dma((16, 2)),
            dma((KRYLOV, len(WIRE), 2)),
            dma((KRYLOV, len(WIRE), 2)),
            dma((KRYLOV, 8, 2)),
            dma((KRYLOV, 8, 2)),
            dma((KRYLOV, 3)),
            dma((KRYLOV, 3)),
            dma((2, 16)),
            dma((2, 16)),
            dma((2, 8)),
            dma((2, 8)),
        ]
        + [vector] * (KRYLOV + 1)
        + [rounded] * (16 * KRYLOV),
        compiler_params=pltpu.CompilerParams(
            collective_id=0, has_side_effects=True, vmem_limit_bytes=60000000
        ),
        name="cycle",
    )(col_block, wall_mask, right_side, relax_rate.reshape(1, -1), drift_speed, upwind_sign, blocks)


def solution(mesh):
    return jax.shard_map(
        per_device,
        mesh=mesh,
        in_specs=(
            P("gx", "gy", "mode"),
            P("mode", None),
            P("mode", None, None, None),
            P("mode"),
            P(None, "mode"),
            P(None, "mode"),
            P("gx", "gy"),
        ),
        out_specs=(P("gx", "gy", "mode"), P()),
        check_vma=False,
    )
```

```python
import functools

import jax
import jax.numpy as jnp
from jax import lax
from jax.experimental import pallas as pl
from jax.experimental.pallas import tpu as pltpu
from jax.sharding import PartitionSpec as P

KRYLOV = 3
MESH = pl.DeviceIdType.MESH
LANES = 128
QUARTERS = 4

epsilon = 1e-12

WIRE = ("A1", "A3", "Z0", "A2", "B", "Z", "C2")
PLACES = [(dz, dy) for dz in range(2) for dy in range(4)]


def least_squares(upper, initial, zero):
    target = [initial] + [zero for row_index in range(KRYLOV)]
    cosines = []
    sines = []
    for col_index in range(KRYLOV):
        for row_index in range(col_index):
            first = upper[row_index][col_index]
            second = upper[row_index + 1][col_index]
            upper[row_index][col_index] = cosines[row_index] * first + sines[row_index] * second
            upper[row_index + 1][col_index] = cosines[row_index] * second - sines[row_index] * first
        first = upper[col_index][col_index]
        second = upper[col_index + 1][col_index]
        radius = jnp.sqrt(first * first + second * second)
        cosine = first / radius
        sine_value = second / radius
        upper[col_index][col_index] = radius
        target[col_index + 1] = -sine_value * target[col_index]
        target[col_index] = cosine * target[col_index]
        cosines.append(cosine)
        sines.append(sine_value)
    combo = [None] * KRYLOV
    for row_index in reversed(range(KRYLOV)):
        running = target[row_index]
        for col_index in range(row_index + 1, KRYLOV):
            running = running - upper[row_index][col_index] * combo[col_index]
        combo[row_index] = running / upper[row_index][row_index]
    return combo


def gram_schmidt(gram, shift, initial):
    size = KRYLOV + 1

    def inner(first, second):
        total = None
        for i in range(size):
            if first[i] is None:
                continue
            row = None
            for k in range(size):
                if second[k] is None:
                    continue
                term = gram[min(i, k)][max(i, k)] * second[k]
                row = term if row is None else row + term
            term = first[i] * row
            total = term if total is None else total + term
        return total

    one = jnp.ones_like(initial)
    zero = jnp.zeros_like(initial)
    basis = [[one, None, None, None]]
    hessenberg = [[zero for col in range(KRYLOV)] for row in range(size)]
    for section in range(KRYLOV):
        current = basis[section]
        mapped = [None] * size
        for i in range(size):
            if current[i] is not None:
                own = shift * current[i]
                mapped[i] = own if mapped[i] is None else mapped[i] + own
                mapped[i + 1] = current[i]
        coefficients = [inner(basis[i], mapped) for i in range(section + 1)]
        for i in range(section + 1):
            hessenberg[i][section] = coefficients[i]
            for k in range(size):
                if basis[i][k] is not None:
                    mapped[k] = mapped[k] - coefficients[i] * basis[i][k]
        length = jnp.sqrt(jnp.maximum(inner(mapped, mapped), 0.0) + epsilon)
        hessenberg[section + 1][section] = length
        basis.append([None if value is None else value / length for value in mapped])
    combo = least_squares([list(row) for row in hessenberg], initial, zero)
    weights = []
    for k in range(KRYLOV):
        total = None
        for section in range(KRYLOV):
            if basis[section][k] is not None:
                term = combo[section] * basis[section][k]
                total = term if total is None else total + term
        weights.append(total)
    return hessenberg, weights


def kernel(
    col_hbm,
    wall_hbm,
    right_hbm,
    relax_hbm,
    drift_hbm,
    sign_hbm,
    blocks_ref,
    out_ref,
    hess_ref,
    col_ref,
    wall_ref,
    right_ref,
    relax_ref,
    drift_ref,
    sign_ref,
    weights,
    tile_one,
    tile_two,
    gather_one,
    gather_two,
    face_out,
    face_in,
    open_ref,
    in_sem,
    w_sem,
    bulk_send,
    bulk_recv,
    pass_send,
    pass_recv,
    face_send,
    face_recv,
    one_send,
    one_recv,
    two_send,
    two_recv,
    *slots,
):
    krylov = slots[: KRYLOV + 1]
    held = [
        {(dz, dy, dc): slots[KRYLOV + 1 + 16 * j + 8 * dc + 4 * dz + dy] for dz, dy in PLACES for dc in range(2)}
        for j in range(KRYLOV)
    ]
    local_blocks = col_ref.shape[0]
    ends = [-(-local_blocks * (q + 1) // QUARTERS) for q in range(QUARTERS)]
    starts = [0] + ends[:-1]
    parts = [pl.ds(start, end - start) for start, end in zip(starts, ends)]

    mode = lax.axis_index("mode")
    gx = lax.axis_index("gx")
    gy = lax.axis_index("gy")
    zh = mode // 8
    y = (mode // 2) % 4
    core = mode % 2
    z = zh * 2 + gx

    def mode_of(dz, dy, dc):
        return lax.rem(zh + dz, 2) * 8 + lax.rem(y + dy, 4) * 2 + lax.rem(core + dc, 2)

    def lanes_of(b):
        return pl.ds(pl.multiple_of(b * LANES, LANES), LANES)

    def weight_copies(dz, dy, dc):
        owner = mode_of(dz, dy, dc)
        place = 8 * dc + 4 * dz + dy
        return [
            pltpu.make_async_copy(
                blocks_ref.at[:, owner * 2 + s],
                weights.at[place, :, :, pl.ds(s * LANES, LANES)],
                w_sem.at[place, s],
            )
            for s in range(2)
        ]

    order = [
        (0, 0, 0), (0, 0, 1), (0, 1, 0), (0, 3, 0), (1, 0, 0), (0, 1, 1), (0, 3, 1), (1, 0, 1),
        (0, 2, 0), (0, 2, 1), (1, 1, 0), (1, 3, 0), (1, 1, 1), (1, 3, 1), (1, 2, 0), (1, 2, 1),
    ]
    ring = []
    for d in range(1, 8):
        z_to = lax.rem(z + d // 2, 4)
        ring.append({"mode": z_to // 2 * 8 + y * 2 + lax.rem(core + d % 2, 2), "gx": lax.rem(z_to, 2)})
    plane = [
        {"mode": zh * 8 + lax.rem(y + d // 4, 4) * 2 + core, "gy": lax.rem(gy + d % 4, 4)} for d in range(1, 16)
    ]
    barrier = pltpu.get_barrier_semaphore()
    for partner in plane + ring:
        pl.semaphore_signal(barrier, inc=1, device_id=partner, device_id_type=MESH)

    inputs = [
        pltpu.make_async_copy(source, target, in_sem.at[index])
        for index, (source, target) in enumerate(
            (
                (right_hbm, right_ref),
                (relax_hbm, relax_ref),
                (drift_hbm, drift_ref),
                (sign_hbm, sign_ref),
                (wall_hbm, wall_ref),
                (col_hbm, col_ref),
            )
        )
    ]
    for copy in inputs:
        copy.start()
    for place in order:
        for copy in weight_copies(*place):
            copy.start()
    for copy in inputs:
        copy.wait()

    def norm_block(b, carry):
        plain, weighted = carry
        lanes = lanes_of(b)
        diagonal = relax_ref[lanes][None, :] + drift_ref[0:1, lanes] + drift_ref[1:2, lanes]
        for x in range(8):
            value = right_ref[x, :, lanes]
            square = value * value
            plain = plain + square
            weighted = weighted + square * diagonal
        return plain, weighted

    empty = jnp.zeros((8, LANES), jnp.float32)
    plain, weighted = lax.fori_loop(0, local_blocks, norm_block, (empty, empty))
    for x in range(8):
        for cell in range(8):
            open_ref[pl.ds(x * 8 + cell, 1), :] = jnp.full(
                (1, LANES), (1 - wall_ref[x, cell]).astype(jnp.float32), jnp.float32
            )

    pl.semaphore_wait(barrier, 22)

    lane = lax.broadcasted_iota(jnp.int32, (1, LANES), 1)

    def exchanged(which, value, partners, me, count, tile, slots_of, send, recv):
        tile[which] = value
        slots_of[which, me] = value
        copies = [
            pltpu.make_async_remote_copy(
                src_ref=tile.at[which],
                dst_ref=slots_of.at[which, me],
                send_sem=send.at[which, index],
                recv_sem=recv.at[which, index],
                device_id=partner,
                device_id_type=MESH,
            )
            for index, partner in enumerate(partners)
        ]
        for copy in copies:
            copy.start()
        for copy in copies:
            copy.wait()
        total = slots_of[which, 0]
        for source in range(1, count):
            total = total + slots_of[which, source]
        return total

    def summed(which, partials):
        packed = jnp.zeros((1, LANES), jnp.float32)
        for k, partial in enumerate(partials):
            own = jnp.sum(jnp.sum(partial, axis=0, keepdims=True), axis=1, keepdims=True)
            packed = jnp.where(lane == k, own, packed)
        packed = exchanged(which, packed, ring, z * 2 + core, 8, tile_one, gather_one, one_send, one_recv)
        packed = exchanged(which, packed, plane, y * 4 + gy, 16, tile_two, gather_two, two_send, two_recv)
        return [
            jnp.broadcast_to(jnp.sum(jnp.where(lane == k, packed, 0.0), axis=1, keepdims=True), (1, LANES))
            for k in range(len(partials))
        ]

    squared, diagonal = summed(0, [plain, weighted])
    initial = jnp.sqrt(squared + epsilon)
    shift = diagonal / (squared + epsilon)

    def first_block(b, carry):
        lanes = lanes_of(b)
        value = (right_ref[:, :, lanes] / initial).reshape(64, LANES)
        krylov[0][b] = value
        held[0][0, 0, 0][b] = value.astype(jnp.bfloat16)
        return carry

    lax.fori_loop(0, local_blocks, first_block, 0)

    sends = []
    rows8 = lax.broadcasted_iota(jnp.int32, (8, LANES), 0)
    grams = {}

    for j in range(KRYLOV):
        x = held[j]
        now = krylov[j]
        later = krylov[j + 1]

        below, above, across, beside = mode_of(0, 3, 0), mode_of(0, 1, 0), mode_of(1, 0, 0), mode_of(0, 0, 1)

        def route(name, q):
            first = q < 2
            return {
                "A1": ((0, 0), (0, 1), below),
                "A3": ((0, 0), (0, 3), above),
                "Z0": ((0, 0), (1, 0), across),
                "A2": ((0, 1), (0, 2), below) if first else ((0, 3), (0, 2), above),
                "B": ((1, 0), (1, 3), above) if first else ((1, 0), (1, 1), below),
                "Z": ((0, 1), (1, 1), across) if first else ((0, 3), (1, 3), across),
                "C2": ((1, 3), (1, 2), above) if first else ((1, 1), (1, 2), below),
            }[name]

        def copy_of(name, q):
            source, target, to = route(name, q)
            index = WIRE.index(name)
            return pltpu.make_async_remote_copy(
                src_ref=x[source[0], source[1], 0].at[parts[q]],
                dst_ref=x[target[0], target[1], 0].at[parts[q]],
                send_sem=bulk_send.at[j, index],
                recv_sem=bulk_recv.at[j, index, q],
                device_id={"mode": to},
                device_id_type=MESH,
            )

        def passing(place, part=None):
            dz, dy = place
            source, target = x[dz, dy, 0], x[dz, dy, 1]
            return pltpu.make_async_remote_copy(
                src_ref=source if part is None else source.at[part],
                dst_ref=target if part is None else target.at[part],
                send_sem=pass_send.at[j, 4 * dz + dy],
                recv_sem=pass_recv.at[j, 4 * dz + dy],
                device_id={"mode": beside},
                device_id_type=MESH,
            )

        def sent_all(index):
            whole = x[0, 0, 0]
            return pltpu.make_async_remote_copy(
                src_ref=whole,
                dst_ref=whole,
                send_sem=bulk_send.at[j, index],
                recv_sem=bulk_recv.at[j, index, 0],
                device_id={"mode": beside},
                device_id_type=MESH,
            )

        def start(copy):
            copy.start()
            sends.append(copy)

        following = {
            ("A1", 0): ("A2", "Z"), ("A1", 1): ("A2", "Z"), ("A3", 2): ("A2", "Z"), ("A3", 3): ("A2", "Z"),
            ("Z0", 0): ("B",), ("Z0", 1): ("B",), ("Z0", 2): ("B",), ("Z0", 3): ("B",),
            ("B", 0): ("C2",), ("B", 1): ("C2",), ("B", 2): ("C2",), ("B", 3): ("C2",),
        }

        def take(name, *quarters):
            for q in quarters:
                copy_of(name, q).wait_recv()
                for after in following.get((name, q), ()):
                    copy_of(after, q).start()
                passing(route(name, q)[1], parts[q]).start()

        def send_own(quarters):
            for q in quarters:
                copy_of("A1", q).start()
                copy_of("A3", q).start()
                copy_of("Z0", (0, 2, 1, 3)[q]).start()
                passing((0, 0), parts[q]).start()

        send_own(range(QUARTERS))
        sends.extend(sent_all(index) for index in range(len(WIRE)))
        sends.extend(passing(place) for place in PLACES)

        def face_block(b, carry):
            low, high = now[b, 0:8, :] * open_ref[0:8, :], now[b, 56:64, :] * open_ref[56:64, :]
            face_out[j, 0, b] = jnp.where(gx == 0, high, low)
            for cell in range(8):
                value = now[b, 8 * cell : 8 * cell + 8, :] * open_ref[8 * cell : 8 * cell + 8, :]
                face_out[j, 1, b, pl.ds(cell, 1), :] = value[7:8, :]
                face_out[j, 2, b, pl.ds(cell, 1), :] = value[0:1, :]
            return carry

        lax.fori_loop(0, local_blocks, face_block, 0)
        faces = []
        for side, to in (
            (0, {"gx": lax.rem(gx + 1, 2)}),
            (1, {"gy": lax.rem(gy + 1, 4)}),
            (2, {"gy": lax.rem(gy + 3, 4)}),
        ):
            copy = pltpu.make_async_remote_copy(
                src_ref=face_out.at[j, side],
                dst_ref=face_in.at[j, side],
                send_sem=face_send.at[j, side],
                recv_sem=face_recv.at[j, side],
                device_id=to,
                device_id_type=MESH,
            )
            start(copy)
            faces.append(copy)

        def product(place, b):
            owner = mode_of(*place)
            first, second = (
                jnp.clip(col_ref[b, owner * 2 + s] - owner * local_blocks, 0, local_blocks - 1) for s in range(2)
            )
            ref = x[place]
            picked = jnp.concatenate([ref[first], ref[second]], axis=1)
            matrix = weights[8 * place[2] + 4 * place[0] + place[1], b]
            return lax.dot_general(picked, matrix, (((1,), (1,)), ((), ())), preferred_element_type=jnp.float32)

        def ready(place):
            if j == 0:
                for copy in weight_copies(*place):
                    copy.wait()
            if place[2] == 1:
                passing(place[:2]).wait_recv()

        def compute(place):
            ready(place)

            def block(b, carry):
                later[b] = later[b] - product(place, b)
                return carry

            lax.fori_loop(0, local_blocks, block, 0, unroll=True)

        def compute_first(place):
            ready(place)

            def block(b, carry):
                later[b] = -product(place, b)
                return carry

            lax.fori_loop(0, local_blocks, block, 0, unroll=True)

        def local_terms():
            for copy in faces:
                copy.wait_recv()

            def block(b, carry):
                lanes = lanes_of(b)
                relax = relax_ref[lanes][None, :] - shift
                speed_first, speed_second = drift_ref[0:1, lanes], drift_ref[1:2, lanes]
                to_higher_first = sign_ref[0:1, lanes] == 1
                to_higher_second = sign_ref[1:2, lanes] == 1
                edge = face_in[j, 0, b]
                values = [now[b, 8 * cell : 8 * cell + 8, :] for cell in range(8)]
                masked = [values[cell] * open_ref[8 * cell : 8 * cell + 8, :] for cell in range(8)]
                west = [jnp.where(gx == 1, edge, 0.0)] + masked[:7]
                east = masked[1:] + [jnp.where(gx == 0, edge, 0.0)]
                for cell in range(8):
                    rows = slice(8 * cell, 8 * cell + 8)
                    from_low = jnp.where(gy > 0, face_in[j, 1, b, pl.ds(cell, 1), :], 0.0)
                    from_high = jnp.where(gy < 3, face_in[j, 2, b, pl.ds(cell, 1), :], 0.0)
                    south = jnp.where(rows8 == 0, from_low, pltpu.roll(masked[cell], 1, 0))
                    north = jnp.where(rows8 == 7, from_high, pltpu.roll(masked[cell], 7, 0))
                    upstream_first = jnp.where(to_higher_first, west[cell], east[cell])
                    upstream_second = jnp.where(to_higher_second, south, north)
                    value = values[cell]
                    term = speed_first * (value - upstream_first) + speed_second * (value - upstream_second)
                    later[b, rows, :] = later[b, rows, :] + (relax * value + term)
                return carry

            lax.fori_loop(0, local_blocks, block, 0)

        def dots_with(k):
            def block(b, carry):
                totals = list(carry)
                for cell in range(8):
                    rows = slice(8 * cell, 8 * cell + 8)
                    value = krylov[k][b, rows, :]
                    for i in range(k + 1):
                        totals[i] = totals[i] + krylov[i][b, rows, :] * value
                return tuple(totals)

            totals = lax.fori_loop(0, local_blocks, block, tuple(empty for i in range(k + 1)))
            for i in range(k + 1):
                grams[i, k] = totals[i]

        compute_first((0, 0, 0))
        compute((0, 0, 1))
        take("A1", 0)
        take("A3", 0)
        take("Z0", 0)
        take("A1", 1)
        take("A3", 1)
        take("Z0", 2)
        dots_with(j)
        take("A1", 2)
        take("A3", 2)
        take("Z0", 1)
        take("A1", 3)
        take("A3", 3)
        take("Z0", 3)
        compute((0, 1, 0))
        take("B", 0)
        take("A2", 0)
        compute((0, 3, 0))
        compute((1, 0, 0))
        take("A2", 1, 2)
        take("Z", 0)
        compute((0, 1, 1))
        compute((0, 3, 1))
        take("B", 1, 2)
        take("Z", 1)
        compute((1, 0, 1))
        local_terms()
        take("A2", 3)
        take("B", 3)
        take("Z", 2)
        compute((0, 2, 0))
        compute((0, 2, 1))
        take("C2", 0)
        take("Z", 3)
        take("C2", 2)
        compute((1, 1, 0))
        compute((1, 3, 0))
        take("C2", 1, 3)
        compute((1, 1, 1))
        compute((1, 3, 1))
        compute((1, 2, 0))
        place = (1, 2, 1)
        ready(place)
        if j < KRYLOV - 1:
            nearby = held[j + 1][0, 0, 0]

            def last_block(b, carry):
                value = later[b] - product(place, b)
                later[b] = value
                nearby[b] = value.astype(jnp.bfloat16)
                return carry

            lax.fori_loop(0, local_blocks, last_block, 0, unroll=True)
        else:

            def final_block(b, carry):
                totals = list(carry)
                value = later[b] - product(place, b)
                for cell in range(8):
                    rows = slice(8 * cell, 8 * cell + 8)
                    part = value[rows, :]
                    for i in range(KRYLOV):
                        totals[i] = totals[i] + krylov[i][b, rows, :] * part
                    totals[KRYLOV] = totals[KRYLOV] + part * part
                return tuple(totals)

            totals = lax.fori_loop(0, local_blocks, final_block, tuple(empty for i in range(KRYLOV + 1)), unroll=True)
            for i in range(KRYLOV + 1):
                grams[i, KRYLOV] = totals[i]

    pairs = [(i, k) for k in range(KRYLOV + 1) for i in range(k + 1)]
    sums = dict(zip(pairs, summed(1, [grams[pair] for pair in pairs])))
    gram = [[sums.get((i, k)) for k in range(KRYLOV + 1)] for i in range(KRYLOV + 1)]
    hessenberg, factors = gram_schmidt(gram, shift, initial)

    def out_block(b, carry):
        lanes = lanes_of(b)
        value = factors[0] * krylov[0][b]
        for k in range(1, KRYLOV):
            value = value + factors[k] * krylov[k][b]
        out_ref[:, :, lanes] = value.reshape(8, 8, LANES)
        return carry

    lax.fori_loop(0, local_blocks, out_block, 0)
    columns = lax.broadcasted_iota(jnp.int32, (8, LANES), 1)
    tile = empty
    for i in range(KRYLOV + 1):
        for k in range(KRYLOV):
            tile = jnp.where((rows8 == i) & (columns == k), hessenberg[i][k], tile)
    hess_ref[...] = tile[: KRYLOV + 1, :KRYLOV]
    for copy in sends:
        copy.wait_send()


def per_device(right_side, col_block, blocks, relax_rate, drift_speed, upwind_sign, wall_mask):
    cells_first, cells_second, local_modes = right_side.shape
    cells = cells_first * cells_second
    local_blocks = col_block.shape[0]
    block = blocks.shape[2]
    vector = pltpu.VMEM((local_blocks, cells, block), jnp.float32)
    rounded = pltpu.VMEM((local_blocks, cells, block), jnp.bfloat16)
    dma = pltpu.SemaphoreType.DMA
    vmem = pl.BlockSpec(memory_space=pltpu.VMEM)
    return pl.pallas_call(
        kernel,
        out_shape=(
            jax.ShapeDtypeStruct(right_side.shape, jnp.float32),
            jax.ShapeDtypeStruct((KRYLOV + 1, KRYLOV), jnp.float32),
        ),
        in_specs=[pl.BlockSpec(memory_space=pl.ANY)] * 7,
        out_specs=(vmem, vmem),
        scratch_shapes=[
            pltpu.SMEM(col_block.shape, jnp.int32),
            pltpu.SMEM(wall_mask.shape, jnp.int32),
            pltpu.VMEM(right_side.shape, jnp.float32),
            pltpu.VMEM(relax_rate.shape, jnp.float32),
            pltpu.VMEM(drift_speed.shape, jnp.float32),
            pltpu.VMEM(upwind_sign.shape, jnp.int32),
            pltpu.VMEM((16, local_blocks, block, 2 * block), jnp.bfloat16),
            pltpu.VMEM((2, 1, LANES), jnp.float32),
            pltpu.VMEM((2, 1, LANES), jnp.float32),
            pltpu.VMEM((2, 8, 1, LANES), jnp.float32),
            pltpu.VMEM((2, 16, 1, LANES), jnp.float32),
            pltpu.VMEM((KRYLOV, 3, local_blocks, 8, LANES), jnp.float32),
            pltpu.VMEM((KRYLOV, 3, local_blocks, 8, LANES), jnp.float32),
            pltpu.VMEM((cells, LANES), jnp.float32),
            dma((6,)),
            dma((16, 2)),
            dma((KRYLOV, len(WIRE))),
            dma((KRYLOV, len(WIRE), QUARTERS)),
            dma((KRYLOV, len(PLACES))),
            dma((KRYLOV, len(PLACES))),
            dma((KRYLOV, 3)),
            dma((KRYLOV, 3)),
            dma((2, 7)),
            dma((2, 7)),
            dma((2, 15)),
            dma((2, 15)),
        ]
        + [vector] * (KRYLOV + 1)
        + [rounded] * (16 * KRYLOV),
        compiler_params=pltpu.CompilerParams(
            collective_id=0, has_side_effects=True, vmem_limit_bytes=60000000
        ),
        name="cycle",
    )(col_block, wall_mask, right_side, relax_rate, drift_speed, upwind_sign, blocks)


def solution(mesh):
    return jax.shard_map(
        per_device,
        mesh=mesh,
        in_specs=(
            P("gx", "gy", "mode"),
            P("mode", None),
            P("mode", None, None, None),
            P("mode"),
            P(None, "mode"),
            P(None, "mode"),
            P("gx", "gy"),
        ),
        out_specs=(P("gx", "gy", "mode"), P()),
        check_vma=False,
    )
```

```python
import functools

import jax
import jax.numpy as jnp
from jax import lax
from jax.experimental import pallas as pl
from jax.experimental.pallas import tpu as pltpu
from jax.sharding import PartitionSpec as P

KRYLOV = 3
MESH = pl.DeviceIdType.MESH
LANES = 128
QUARTERS = 4

epsilon = 1e-12

WIRE = ("A1", "A3", "Z0", "A2", "B", "Z", "C2")
PLACES = [(dz, dy) for dz in range(2) for dy in range(4)]


def least_squares(upper, initial, zero):
    target = [initial] + [zero for row_index in range(KRYLOV)]
    cosines = []
    sines = []
    for col_index in range(KRYLOV):
        for row_index in range(col_index):
            first = upper[row_index][col_index]
            second = upper[row_index + 1][col_index]
            upper[row_index][col_index] = cosines[row_index] * first + sines[row_index] * second
            upper[row_index + 1][col_index] = cosines[row_index] * second - sines[row_index] * first
        first = upper[col_index][col_index]
        second = upper[col_index + 1][col_index]
        radius = jnp.sqrt(first * first + second * second)
        cosine = first / radius
        sine_value = second / radius
        upper[col_index][col_index] = radius
        target[col_index + 1] = -sine_value * target[col_index]
        target[col_index] = cosine * target[col_index]
        cosines.append(cosine)
        sines.append(sine_value)
    combo = [None] * KRYLOV
    for row_index in reversed(range(KRYLOV)):
        running = target[row_index]
        for col_index in range(row_index + 1, KRYLOV):
            running = running - upper[row_index][col_index] * combo[col_index]
        combo[row_index] = running / upper[row_index][row_index]
    return combo


def gram_schmidt(gram, shift, initial):
    size = KRYLOV + 1

    def inner(first, second):
        total = None
        for i in range(size):
            if first[i] is None:
                continue
            row = None
            for k in range(size):
                if second[k] is None:
                    continue
                term = gram[min(i, k)][max(i, k)] * second[k]
                row = term if row is None else row + term
            term = first[i] * row
            total = term if total is None else total + term
        return total

    zero = jnp.zeros_like(initial)
    basis = [[1.0 / initial, None, None, None]]
    hessenberg = [[zero for col in range(KRYLOV)] for row in range(size)]
    for section in range(KRYLOV):
        current = basis[section]
        mapped = [None] * size
        for i in range(size):
            if current[i] is not None:
                own = shift * current[i]
                mapped[i] = own if mapped[i] is None else mapped[i] + own
                mapped[i + 1] = current[i]
        coefficients = [inner(basis[i], mapped) for i in range(section + 1)]
        for i in range(section + 1):
            hessenberg[i][section] = coefficients[i]
            for k in range(size):
                if basis[i][k] is not None:
                    mapped[k] = mapped[k] - coefficients[i] * basis[i][k]
        length = jnp.sqrt(jnp.maximum(inner(mapped, mapped), 0.0) + epsilon)
        hessenberg[section + 1][section] = length
        basis.append([None if value is None else value / length for value in mapped])
    combo = least_squares([list(row) for row in hessenberg], initial, zero)
    weights = []
    for k in range(KRYLOV):
        total = None
        for section in range(KRYLOV):
            if basis[section][k] is not None:
                term = combo[section] * basis[section][k]
                total = term if total is None else total + term
        weights.append(total)
    return hessenberg, weights


def kernel(
    col_hbm,
    wall_hbm,
    right_hbm,
    relax_hbm,
    drift_hbm,
    sign_hbm,
    blocks_ref,
    out_ref,
    hess_ref,
    col_ref,
    wall_ref,
    right_ref,
    relax_ref,
    drift_ref,
    sign_ref,
    weights,
    tile_one,
    tile_two,
    gather_one,
    gather_two,
    face_out,
    face_in,
    open_ref,
    in_sem,
    w_sem,
    bulk_send,
    bulk_recv,
    pass_send,
    pass_recv,
    face_send,
    face_recv,
    one_send,
    one_recv,
    two_send,
    two_recv,
    *slots,
):
    krylov = slots[: KRYLOV + 1]
    held = [
        {(dz, dy, dc): slots[KRYLOV + 1 + 16 * j + 8 * dc + 4 * dz + dy] for dz, dy in PLACES for dc in range(2)}
        for j in range(KRYLOV)
    ]
    local_blocks = col_ref.shape[0]
    ends = [-(-local_blocks * (q + 1) // QUARTERS) for q in range(QUARTERS)]
    starts = [0] + ends[:-1]
    parts = [pl.ds(start, end - start) for start, end in zip(starts, ends)]

    mode = lax.axis_index("mode")
    gx = lax.axis_index("gx")
    gy = lax.axis_index("gy")
    zh = mode // 8
    y = (mode // 2) % 4
    core = mode % 2
    z = zh * 2 + gx

    def mode_of(dz, dy, dc):
        return lax.rem(zh + dz, 2) * 8 + lax.rem(y + dy, 4) * 2 + lax.rem(core + dc, 2)

    def lanes_of(b):
        return pl.ds(pl.multiple_of(b * LANES, LANES), LANES)

    def weight_copies(dz, dy, dc):
        owner = mode_of(dz, dy, dc)
        place = 8 * dc + 4 * dz + dy
        return [
            pltpu.make_async_copy(
                blocks_ref.at[:, owner * 2 + s],
                weights.at[place, :, :, pl.ds(s * LANES, LANES)],
                w_sem.at[place, s],
            )
            for s in range(2)
        ]

    order = [
        (0, 0, 0), (0, 0, 1), (0, 1, 0), (0, 3, 0), (1, 0, 0), (0, 1, 1), (0, 3, 1), (1, 0, 1),
        (0, 2, 0), (0, 2, 1), (1, 1, 0), (1, 3, 0), (1, 1, 1), (1, 3, 1), (1, 2, 0), (1, 2, 1),
    ]
    ring = []
    for d in range(1, 8):
        z_to = lax.rem(z + d // 2, 4)
        ring.append({"mode": z_to // 2 * 8 + y * 2 + lax.rem(core + d % 2, 2), "gx": lax.rem(z_to, 2)})
    plane = [
        {"mode": zh * 8 + lax.rem(y + d // 4, 4) * 2 + core, "gy": lax.rem(gy + d % 4, 4)} for d in range(1, 16)
    ]
    barrier = pltpu.get_barrier_semaphore()
    for partner in plane + ring:
        pl.semaphore_signal(barrier, inc=1, device_id=partner, device_id_type=MESH)

    inputs = [
        pltpu.make_async_copy(source, target, in_sem.at[index])
        for index, (source, target) in enumerate(
            (
                (right_hbm, right_ref),
                (relax_hbm, relax_ref),
                (drift_hbm, drift_ref),
                (sign_hbm, sign_ref),
                (wall_hbm, wall_ref),
                (col_hbm, col_ref),
            )
        )
    ]
    for copy in inputs:
        copy.start()
    for place in order:
        for copy in weight_copies(*place):
            copy.start()
    for copy in inputs:
        copy.wait()

    def norm_block(b, carry):
        plain, weighted = carry
        lanes = lanes_of(b)
        diagonal = relax_ref[lanes][None, :] + drift_ref[0:1, lanes] + drift_ref[1:2, lanes]
        for x in range(8):
            value = right_ref[x, :, lanes]
            square = value * value
            plain = plain + square
            weighted = weighted + square * diagonal
        value = right_ref[:, :, lanes].reshape(64, LANES)
        krylov[0][b] = value
        held[0][0, 0, 0][b] = value.astype(jnp.bfloat16)
        return plain, weighted

    empty = jnp.zeros((8, LANES), jnp.float32)
    plain, weighted = lax.fori_loop(0, local_blocks, norm_block, (empty, empty))
    for x in range(8):
        for cell in range(8):
            open_ref[pl.ds(x * 8 + cell, 1), :] = jnp.full(
                (1, LANES), (1 - wall_ref[x, cell]).astype(jnp.float32), jnp.float32
            )

    pl.semaphore_wait(barrier, 22)

    lane = lax.broadcasted_iota(jnp.int32, (1, LANES), 1)

    stages = (
        (ring, z * 2 + core, 8, tile_one, gather_one, one_send, one_recv),
        (plane, y * 4 + gy, 16, tile_two, gather_two, two_send, two_recv),
    )

    def copies_of(which, stage):
        partners, me, _, tile, places, send, recv = stages[stage]
        return [
            pltpu.make_async_remote_copy(
                src_ref=tile.at[which],
                dst_ref=places.at[which, me],
                send_sem=send.at[which, index],
                recv_sem=recv.at[which, index],
                device_id=partner,
                device_id_type=MESH,
            )
            for index, partner in enumerate(partners)
        ]

    def post(which, stage, value):
        _, me, _, tile, places, _, _ = stages[stage]
        tile[which] = value
        places[which, me] = value
        for copy in copies_of(which, stage):
            copy.start()

    def collect(which, stage):
        _, _, count, _, places, _, _ = stages[stage]
        for copy in copies_of(which, stage):
            copy.wait()
        total = places[which, 0]
        for source in range(1, count):
            total = total + places[which, source]
        return total

    def pack(partials):
        packed = jnp.zeros((1, LANES), jnp.float32)
        for k, partial in enumerate(partials):
            own = jnp.sum(jnp.sum(partial, axis=0, keepdims=True), axis=1, keepdims=True)
            packed = jnp.where(lane == k, own, packed)
        return packed

    def unpack(packed, count):
        return [
            jnp.broadcast_to(jnp.sum(jnp.where(lane == k, packed, 0.0), axis=1, keepdims=True), (1, LANES))
            for k in range(count)
        ]

    post(0, 0, pack([plain, weighted]))
    sends = []
    rows8 = lax.broadcasted_iota(jnp.int32, (8, LANES), 0)
    grams = {}

    def start(copy):
        copy.start()
        sends.append(copy)

    def gather_of(j):
        x = held[j]
        below, above, across, beside = mode_of(0, 3, 0), mode_of(0, 1, 0), mode_of(1, 0, 0), mode_of(0, 0, 1)

        def route(name, q):
            even = q % 2 == 0
            return {
                "A1": ((0, 0), (0, 1), below),
                "A3": ((0, 0), (0, 3), above),
                "Z0": ((0, 0), (1, 0), across),
                "A2": ((0, 1), (0, 2), below) if even else ((0, 3), (0, 2), above),
                "B": ((1, 0), (1, 3), above) if even else ((1, 0), (1, 1), below),
                "Z": ((0, 1), (1, 1), across) if even else ((0, 3), (1, 3), across),
                "C2": ((1, 3), (1, 2), above) if even else ((1, 1), (1, 2), below),
            }[name]

        def copy_of(name, q):
            source, target, to = route(name, q)
            index = WIRE.index(name)
            return pltpu.make_async_remote_copy(
                src_ref=x[source[0], source[1], 0].at[parts[q]],
                dst_ref=x[target[0], target[1], 0].at[parts[q]],
                send_sem=bulk_send.at[j, index],
                recv_sem=bulk_recv.at[j, index, q],
                device_id={"mode": to},
                device_id_type=MESH,
            )

        def passing(place, part=None):
            dz, dy = place
            source, target = x[dz, dy, 0], x[dz, dy, 1]
            return pltpu.make_async_remote_copy(
                src_ref=source if part is None else source.at[part],
                dst_ref=target if part is None else target.at[part],
                send_sem=pass_send.at[j, 4 * dz + dy],
                recv_sem=pass_recv.at[j, 4 * dz + dy],
                device_id={"mode": beside},
                device_id_type=MESH,
            )

        def sent_all(index):
            whole = x[0, 0, 0]
            return pltpu.make_async_remote_copy(
                src_ref=whole,
                dst_ref=whole,
                send_sem=bulk_send.at[j, index],
                recv_sem=bulk_recv.at[j, index, 0],
                device_id={"mode": beside},
                device_id_type=MESH,
            )

        following = {("A1", 0): ("A2", "Z"), ("A1", 2): ("A2", "Z"), ("A3", 1): ("A2", "Z"), ("A3", 3): ("A2", "Z")}
        for q in range(QUARTERS):
            following["Z0", q] = ("B",)
            following["B", q] = ("C2",)

        def take(name, *quarters):
            for q in quarters:
                copy_of(name, q).wait_recv()
                for after in following.get((name, q), ()):
                    copy_of(after, q).start()
                passing(route(name, q)[1], parts[q]).start()

        def send_own(q):
            copy_of("A1", q).start()
            copy_of("A3", q).start()
            copy_of("Z0", q).start()
            passing((0, 0), parts[q]).start()

        sends.extend(sent_all(index) for index in range(len(WIRE)))
        sends.extend(passing(place) for place in PLACES)
        return passing, take, send_own

    gathers = [gather_of(j) for j in range(KRYLOV)]
    for q in range(QUARTERS):
        gathers[0][2](q)

    for j in range(KRYLOV):
        x = held[j]
        now = krylov[j]
        later = krylov[j + 1]

        passing, take, _ = gathers[j]

        def face_block(b, carry):
            low, high = now[b, 0:8, :] * open_ref[0:8, :], now[b, 56:64, :] * open_ref[56:64, :]
            face_out[j, 0, b] = jnp.where(gx == 0, high, low)
            for cell in range(8):
                value = now[b, 8 * cell : 8 * cell + 8, :] * open_ref[8 * cell : 8 * cell + 8, :]
                face_out[j, 1, b, pl.ds(cell, 1), :] = value[7:8, :]
                face_out[j, 2, b, pl.ds(cell, 1), :] = value[0:1, :]
            return carry

        lax.fori_loop(0, local_blocks, face_block, 0)
        faces = [
            pltpu.make_async_remote_copy(
                src_ref=face_out.at[j, side],
                dst_ref=face_in.at[j, side],
                send_sem=face_send.at[j, side],
                recv_sem=face_recv.at[j, side],
                device_id=to,
                device_id_type=MESH,
            )
            for side, to in (
                (0, {"gx": lax.rem(gx + 1, 2)}),
                (1, {"gy": lax.rem(gy + 1, 4)}),
                (2, {"gy": lax.rem(gy + 3, 4)}),
            )
        ]
        start(faces[1])
        start(faces[2])

        def product(place, b):
            owner = mode_of(*place)
            first, second = (
                jnp.clip(col_ref[b, owner * 2 + s] - owner * local_blocks, 0, local_blocks - 1) for s in range(2)
            )
            ref = x[place]
            picked = jnp.concatenate([ref[first], ref[second]], axis=1)
            matrix = weights[8 * place[2] + 4 * place[0] + place[1], b]
            return lax.dot_general(picked, matrix, (((1,), (1,)), ((), ())), preferred_element_type=jnp.float32)

        def ready(place):
            if j == 0:
                for copy in weight_copies(*place):
                    copy.wait()
            if place[2] == 1:
                passing(place[:2]).wait_recv()

        def compute(place):
            ready(place)

            def block(b, carry):
                later[b] = later[b] - product(place, b)
                return carry

            lax.fori_loop(0, local_blocks, block, 0, unroll=True)

        def compute_first(place):
            ready(place)

            def block(b, carry):
                later[b] = -product(place, b)
                return carry

            lax.fori_loop(0, local_blocks, block, 0, unroll=True)

        def local_terms():
            for copy in faces[1:]:
                copy.wait_recv()

            def block(b, carry):
                lanes = lanes_of(b)
                relax = relax_ref[lanes][None, :] - shift
                speed_first, speed_second = drift_ref[0:1, lanes], drift_ref[1:2, lanes]
                to_higher_first = sign_ref[0:1, lanes] == 1
                to_higher_second = sign_ref[1:2, lanes] == 1
                values = [now[b, 8 * cell : 8 * cell + 8, :] for cell in range(8)]
                masked = [values[cell] * open_ref[8 * cell : 8 * cell + 8, :] for cell in range(8)]
                west = [empty] + masked[:7]
                east = masked[1:] + [empty]
                for cell in range(8):
                    rows = slice(8 * cell, 8 * cell + 8)
                    from_low = jnp.where(gy > 0, face_in[j, 1, b, pl.ds(cell, 1), :], 0.0)
                    from_high = jnp.where(gy < 3, face_in[j, 2, b, pl.ds(cell, 1), :], 0.0)
                    south = jnp.where(rows8 == 0, from_low, pltpu.roll(masked[cell], 1, 0))
                    north = jnp.where(rows8 == 7, from_high, pltpu.roll(masked[cell], 7, 0))
                    upstream_first = jnp.where(to_higher_first, west[cell], east[cell])
                    upstream_second = jnp.where(to_higher_second, south, north)
                    value = values[cell]
                    term = speed_first * (value - upstream_first) + speed_second * (value - upstream_second)
                    later[b, rows, :] = later[b, rows, :] + (relax * value + term)
                return carry

            lax.fori_loop(0, local_blocks, block, 0)

        def edge_terms():
            faces[0].wait_recv()
            rows = pl.ds(pl.multiple_of((1 - gx) * 56, 8), 8)

            def block(b, carry):
                lanes = lanes_of(b)
                inward = sign_ref[0:1, lanes] == gx
                later[b, rows, :] = later[b, rows, :] - jnp.where(
                    inward, drift_ref[0:1, lanes] * face_in[j, 0, b], 0.0
                )
                return carry

            lax.fori_loop(0, local_blocks, block, 0)

        def dots_with(k):
            def block(b, carry):
                totals = list(carry)
                for cell in range(8):
                    rows = slice(8 * cell, 8 * cell + 8)
                    value = krylov[k][b, rows, :]
                    for i in range(k + 1):
                        totals[i] = totals[i] + krylov[i][b, rows, :] * value
                return tuple(totals)

            totals = lax.fori_loop(0, local_blocks, block, tuple(empty for i in range(k + 1)))
            for i in range(k + 1):
                grams[i, k] = totals[i]

        compute_first((0, 0, 0))
        compute((0, 0, 1))
        take("A1", 0)
        take("A3", 0)
        take("Z0", 0)
        take("A3", 1)
        take("A1", 1)
        take("Z0", 1)
        dots_with(j)
        if j == 0:
            post(0, 1, collect(0, 0))
        take("A1", 2)
        take("A3", 2)
        take("Z0", 2)
        take("A3", 3)
        take("A1", 3)
        take("Z0", 3)
        start(faces[0])
        compute((0, 1, 0))
        take("B", 0)
        take("A2", 0)
        compute((0, 3, 0))
        take("B", 1)
        take("A2", 1)
        compute((1, 0, 0))
        take("Z", 0)
        compute((0, 1, 1))
        take("B", 2)
        take("A2", 2)
        compute((0, 3, 1))
        take("Z", 1)
        compute((1, 0, 1))
        if j == 0:
            squared, diagonal = unpack(collect(0, 1), 2)
            shift = diagonal / (squared + epsilon)
        local_terms()
        take("B", 3)
        take("A2", 3)
        take("Z", 2)
        compute((0, 2, 0))
        compute((0, 2, 1))
        take("C2", 0, 1)
        take("Z", 3)
        compute((1, 1, 0))
        compute((1, 3, 0))
        take("C2", 2)
        compute((1, 1, 1))
        take("C2", 3)
        compute((1, 3, 1))
        edge_terms()
        compute((1, 2, 0))
        place = (1, 2, 1)
        ready(place)
        if j < KRYLOV - 1:
            nearby = held[j + 1][0, 0, 0]

            for q in range(QUARTERS):
                for b in range(starts[q], ends[q]):
                    value = later[b] - product(place, b)
                    later[b] = value
                    nearby[b] = value.astype(jnp.bfloat16)
                gathers[j + 1][2](q)
        else:

            def final_block(b, carry):
                totals = list(carry)
                value = later[b] - product(place, b)
                for cell in range(8):
                    rows = slice(8 * cell, 8 * cell + 8)
                    part = value[rows, :]
                    for i in range(KRYLOV):
                        totals[i] = totals[i] + krylov[i][b, rows, :] * part
                    totals[KRYLOV] = totals[KRYLOV] + part * part
                return tuple(totals)

            totals = lax.fori_loop(0, local_blocks, final_block, tuple(empty for i in range(KRYLOV + 1)), unroll=True)
            for i in range(KRYLOV + 1):
                grams[i, KRYLOV] = totals[i]

    pairs = [(i, k) for k in range(KRYLOV + 1) for i in range(k + 1)]
    post(1, 0, pack([grams[pair] for pair in pairs]))
    post(1, 1, collect(1, 0))
    sums = dict(zip(pairs, unpack(collect(1, 1), len(pairs))))
    gram = [[sums.get((i, k)) for k in range(KRYLOV + 1)] for i in range(KRYLOV + 1)]
    initial = jnp.sqrt(gram[0][0] + epsilon)
    hessenberg, factors = gram_schmidt(gram, shift, initial)

    def out_block(b, carry):
        lanes = lanes_of(b)
        value = factors[0] * krylov[0][b]
        for k in range(1, KRYLOV):
            value = value + factors[k] * krylov[k][b]
        out_ref[:, :, lanes] = value.reshape(8, 8, LANES)
        return carry

    lax.fori_loop(0, local_blocks, out_block, 0)
    columns = lax.broadcasted_iota(jnp.int32, (8, LANES), 1)
    tile = empty
    for i in range(KRYLOV + 1):
        for k in range(KRYLOV):
            tile = jnp.where((rows8 == i) & (columns == k), hessenberg[i][k], tile)
    hess_ref[...] = tile[: KRYLOV + 1, :KRYLOV]
    for copy in sends:
        copy.wait_send()


def per_device(right_side, col_block, blocks, relax_rate, drift_speed, upwind_sign, wall_mask):
    cells_first, cells_second, local_modes = right_side.shape
    cells = cells_first * cells_second
    local_blocks = col_block.shape[0]
    block = blocks.shape[2]
    vector = pltpu.VMEM((local_blocks, cells, block), jnp.float32)
    rounded = pltpu.VMEM((local_blocks, cells, block), jnp.bfloat16)
    dma = pltpu.SemaphoreType.DMA
    vmem = pl.BlockSpec(memory_space=pltpu.VMEM)
    return pl.pallas_call(
        kernel,
        out_shape=(
            jax.ShapeDtypeStruct(right_side.shape, jnp.float32),
            jax.ShapeDtypeStruct((KRYLOV + 1, KRYLOV), jnp.float32),
        ),
        in_specs=[pl.BlockSpec(memory_space=pl.ANY)] * 7,
        out_specs=(vmem, vmem),
        scratch_shapes=[
            pltpu.SMEM(col_block.shape, jnp.int32),
            pltpu.SMEM(wall_mask.shape, jnp.int32),
            pltpu.VMEM(right_side.shape, jnp.float32),
            pltpu.VMEM(relax_rate.shape, jnp.float32),
            pltpu.VMEM(drift_speed.shape, jnp.float32),
            pltpu.VMEM(upwind_sign.shape, jnp.int32),
            pltpu.VMEM((16, local_blocks, block, 2 * block), jnp.bfloat16),
            pltpu.VMEM((2, 1, LANES), jnp.float32),
            pltpu.VMEM((2, 1, LANES), jnp.float32),
            pltpu.VMEM((2, 8, 1, LANES), jnp.float32),
            pltpu.VMEM((2, 16, 1, LANES), jnp.float32),
            pltpu.VMEM((KRYLOV, 3, local_blocks, 8, LANES), jnp.float32),
            pltpu.VMEM((KRYLOV, 3, local_blocks, 8, LANES), jnp.float32),
            pltpu.VMEM((cells, LANES), jnp.float32),
            dma((6,)),
            dma((16, 2)),
            dma((KRYLOV, len(WIRE))),
            dma((KRYLOV, len(WIRE), QUARTERS)),
            dma((KRYLOV, len(PLACES))),
            dma((KRYLOV, len(PLACES))),
            dma((KRYLOV, 3)),
            dma((KRYLOV, 3)),
            dma((2, 7)),
            dma((2, 7)),
            dma((2, 15)),
            dma((2, 15)),
        ]
        + [vector] * (KRYLOV + 1)
        + [rounded] * (16 * KRYLOV),
        compiler_params=pltpu.CompilerParams(
            collective_id=0, has_side_effects=True, vmem_limit_bytes=60000000
        ),
        name="cycle",
    )(col_block, wall_mask, right_side, relax_rate, drift_speed, upwind_sign, blocks)


def solution(mesh):
    return jax.shard_map(
        per_device,
        mesh=mesh,
        in_specs=(
            P("gx", "gy", "mode"),
            P("mode", None),
            P("mode", None, None, None),
            P("mode"),
            P(None, "mode"),
            P(None, "mode"),
            P("gx", "gy"),
        ),
        out_specs=(P("gx", "gy", "mode"), P()),
        check_vma=False,
    )
```

```python
import functools

import jax
import jax.numpy as jnp
from jax import lax
from jax.experimental import pallas as pl
from jax.experimental.pallas import tpu as pltpu
from jax.sharding import PartitionSpec as P

KRYLOV = 3
MESH = pl.DeviceIdType.MESH
LANES = 128
QUARTERS = 4

epsilon = 1e-12

WIRE = ("A1", "A3", "Z0", "A2", "B", "Z", "C2")
PLACES = [(dz, dy) for dz in range(2) for dy in range(4)]


def least_squares(upper, initial, zero):
    target = [initial] + [zero for row_index in range(KRYLOV)]
    cosines = []
    sines = []
    for col_index in range(KRYLOV):
        for row_index in range(col_index):
            first = upper[row_index][col_index]
            second = upper[row_index + 1][col_index]
            upper[row_index][col_index] = cosines[row_index] * first + sines[row_index] * second
            upper[row_index + 1][col_index] = cosines[row_index] * second - sines[row_index] * first
        first = upper[col_index][col_index]
        second = upper[col_index + 1][col_index]
        radius = jnp.sqrt(first * first + second * second)
        cosine = first / radius
        sine_value = second / radius
        upper[col_index][col_index] = radius
        target[col_index + 1] = -sine_value * target[col_index]
        target[col_index] = cosine * target[col_index]
        cosines.append(cosine)
        sines.append(sine_value)
    combo = [None] * KRYLOV
    for row_index in reversed(range(KRYLOV)):
        running = target[row_index]
        for col_index in range(row_index + 1, KRYLOV):
            running = running - upper[row_index][col_index] * combo[col_index]
        combo[row_index] = running / upper[row_index][row_index]
    return combo


def gram_schmidt(gram, shift, initial):
    size = KRYLOV + 1

    def inner(first, second):
        total = None
        for i in range(size):
            if first[i] is None:
                continue
            row = None
            for k in range(size):
                if second[k] is None:
                    continue
                term = gram[min(i, k)][max(i, k)] * second[k]
                row = term if row is None else row + term
            term = first[i] * row
            total = term if total is None else total + term
        return total

    zero = jnp.zeros_like(initial)
    basis = [[1.0 / initial, None, None, None]]
    hessenberg = [[zero for col in range(KRYLOV)] for row in range(size)]
    for section in range(KRYLOV):
        current = basis[section]
        mapped = [None] * size
        for i in range(size):
            if current[i] is not None:
                own = shift * current[i]
                mapped[i] = own if mapped[i] is None else mapped[i] + own
                mapped[i + 1] = current[i]
        coefficients = [inner(basis[i], mapped) for i in range(section + 1)]
        for i in range(section + 1):
            hessenberg[i][section] = coefficients[i]
            for k in range(size):
                if basis[i][k] is not None:
                    mapped[k] = mapped[k] - coefficients[i] * basis[i][k]
        length = jnp.sqrt(jnp.maximum(inner(mapped, mapped), 0.0) + epsilon)
        hessenberg[section + 1][section] = length
        basis.append([None if value is None else value / length for value in mapped])
    combo = least_squares([list(row) for row in hessenberg], initial, zero)
    weights = []
    for k in range(KRYLOV):
        total = None
        for section in range(KRYLOV):
            if basis[section][k] is not None:
                term = combo[section] * basis[section][k]
                total = term if total is None else total + term
        weights.append(total)
    return hessenberg, weights


def kernel(
    col_hbm,
    wall_hbm,
    right_hbm,
    relax_hbm,
    drift_hbm,
    sign_hbm,
    blocks_ref,
    out_ref,
    hess_ref,
    col_ref,
    wall_ref,
    right_ref,
    relax_ref,
    drift_ref,
    sign_ref,
    weights,
    tile_one,
    tile_two,
    gather_one,
    gather_two,
    face_out,
    face_in,
    open_ref,
    in_sem,
    w_sem,
    bulk_send,
    bulk_recv,
    pass_send,
    pass_recv,
    face_send,
    face_recv,
    one_send,
    one_recv,
    two_send,
    two_recv,
    *slots,
):
    krylov = slots[: KRYLOV + 1]
    held = [
        {(dz, dy, dc): slots[KRYLOV + 1 + 16 * j + 8 * dc + 4 * dz + dy] for dz, dy in PLACES for dc in range(2)}
        for j in range(KRYLOV)
    ]
    local_blocks = col_ref.shape[0]
    ends = [-(-local_blocks * (q + 1) // QUARTERS) for q in range(QUARTERS)]
    starts = [0] + ends[:-1]
    parts = [pl.ds(start, end - start) for start, end in zip(starts, ends)]

    mode = lax.axis_index("mode")
    gx = lax.axis_index("gx")
    gy = lax.axis_index("gy")
    zh = mode // 8
    y = (mode // 2) % 4
    core = mode % 2
    z = zh * 2 + gx

    def mode_of(dz, dy, dc):
        return lax.rem(zh + dz, 2) * 8 + lax.rem(y + dy, 4) * 2 + lax.rem(core + dc, 2)

    def lanes_of(b):
        return pl.ds(pl.multiple_of(b * LANES, LANES), LANES)

    def weight_copies(dz, dy, dc):
        owner = mode_of(dz, dy, dc)
        place = 8 * dc + 4 * dz + dy
        return [
            pltpu.make_async_copy(
                blocks_ref.at[:, owner * 2 + s],
                weights.at[place, :, :, pl.ds(s * LANES, LANES)],
                w_sem.at[place, s],
            )
            for s in range(2)
        ]

    order = [
        (0, 0, 0), (0, 0, 1), (0, 1, 0), (0, 3, 0), (1, 0, 0), (0, 1, 1), (0, 3, 1), (1, 0, 1),
        (0, 2, 0), (0, 2, 1), (1, 1, 0), (1, 3, 0), (1, 1, 1), (1, 3, 1), (1, 2, 0), (1, 2, 1),
    ]
    ring = []
    for d in range(1, 8):
        z_to = lax.rem(z + d // 2, 4)
        ring.append({"mode": z_to // 2 * 8 + y * 2 + lax.rem(core + d % 2, 2), "gx": lax.rem(z_to, 2)})
    plane = [
        {"mode": zh * 8 + lax.rem(y + d // 4, 4) * 2 + core, "gy": lax.rem(gy + d % 4, 4)} for d in range(1, 16)
    ]
    barrier = pltpu.get_barrier_semaphore()
    for partner in plane + ring:
        pl.semaphore_signal(barrier, inc=1, device_id=partner, device_id_type=MESH)

    inputs = [
        pltpu.make_async_copy(source, target, in_sem.at[index])
        for index, (source, target) in enumerate(
            (
                (right_hbm, right_ref),
                (relax_hbm, relax_ref),
                (drift_hbm, drift_ref),
                (sign_hbm, sign_ref),
                (wall_hbm, wall_ref),
                (col_hbm, col_ref),
            )
        )
    ]
    for copy in inputs:
        copy.start()
    for place in order:
        for copy in weight_copies(*place):
            copy.start()
    for copy in inputs:
        copy.wait()

    def norm_block(b, carry):
        plain, weighted = carry
        lanes = lanes_of(b)
        diagonal = relax_ref[lanes][None, :] + drift_ref[0:1, lanes] + drift_ref[1:2, lanes]
        for x in range(8):
            value = right_ref[x, :, lanes]
            square = value * value
            plain = plain + square
            weighted = weighted + square * diagonal
        value = right_ref[:, :, lanes].reshape(64, LANES)
        krylov[0][b] = value
        held[0][0, 0, 0][b] = value.astype(jnp.bfloat16)
        return plain, weighted

    empty = jnp.zeros((8, LANES), jnp.float32)
    plain, weighted = lax.fori_loop(0, local_blocks, norm_block, (empty, empty))
    for x in range(8):
        for cell in range(8):
            open_ref[pl.ds(x * 8 + cell, 1), :] = jnp.full(
                (1, LANES), (1 - wall_ref[x, cell]).astype(jnp.float32), jnp.float32
            )

    pl.semaphore_wait(barrier, 22)

    lane = lax.broadcasted_iota(jnp.int32, (1, LANES), 1)

    stages = (
        (ring, z * 2 + core, 8, tile_one, gather_one, one_send, one_recv),
        (plane, y * 4 + gy, 16, tile_two, gather_two, two_send, two_recv),
    )

    def copies_of(which, stage):
        partners, me, _, tile, places, send, recv = stages[stage]
        return [
            pltpu.make_async_remote_copy(
                src_ref=tile.at[which],
                dst_ref=places.at[which, me],
                send_sem=send.at[which, index],
                recv_sem=recv.at[which, index],
                device_id=partner,
                device_id_type=MESH,
            )
            for index, partner in enumerate(partners)
        ]

    def post(which, stage, value):
        _, me, _, tile, places, _, _ = stages[stage]
        tile[which] = value
        places[which, me] = value
        for copy in copies_of(which, stage):
            copy.start()

    def collect(which, stage):
        _, _, count, _, places, _, _ = stages[stage]
        for copy in copies_of(which, stage):
            copy.wait()
        total = places[which, 0]
        for source in range(1, count):
            total = total + places[which, source]
        return total

    def pack(partials):
        packed = jnp.zeros((1, LANES), jnp.float32)
        for k, partial in enumerate(partials):
            own = jnp.sum(jnp.sum(partial, axis=0, keepdims=True), axis=1, keepdims=True)
            packed = jnp.where(lane == k, own, packed)
        return packed

    def unpack(packed, count):
        return [
            jnp.broadcast_to(jnp.sum(jnp.where(lane == k, packed, 0.0), axis=1, keepdims=True), (1, LANES))
            for k in range(count)
        ]

    post(0, 0, pack([plain, weighted]))
    sends = []
    rows8 = lax.broadcasted_iota(jnp.int32, (8, LANES), 0)
    grams = {}

    def start(copy):
        copy.start()
        sends.append(copy)

    def gather_of(j):
        x = held[j]
        below, above, across, beside = mode_of(0, 3, 0), mode_of(0, 1, 0), mode_of(1, 0, 0), mode_of(0, 0, 1)

        def route(name, q):
            even = q % 2 == 0
            return {
                "A1": ((0, 0), (0, 1), below),
                "A3": ((0, 0), (0, 3), above),
                "Z0": ((0, 0), (1, 0), across),
                "A2": ((0, 1), (0, 2), below) if even else ((0, 3), (0, 2), above),
                "B": ((1, 0), (1, 3), above) if even else ((1, 0), (1, 1), below),
                "Z": ((0, 1), (1, 1), across) if even else ((0, 3), (1, 3), across),
                "C2": ((1, 3), (1, 2), above) if even else ((1, 1), (1, 2), below),
            }[name]

        def copy_of(name, q):
            source, target, to = route(name, q)
            index = WIRE.index(name)
            return pltpu.make_async_remote_copy(
                src_ref=x[source[0], source[1], 0].at[parts[q]],
                dst_ref=x[target[0], target[1], 0].at[parts[q]],
                send_sem=bulk_send.at[j, index],
                recv_sem=bulk_recv.at[j, index, q],
                device_id={"mode": to},
                device_id_type=MESH,
            )

        def passing(place, part=None):
            dz, dy = place
            source, target = x[dz, dy, 0], x[dz, dy, 1]
            return pltpu.make_async_remote_copy(
                src_ref=source if part is None else source.at[part],
                dst_ref=target if part is None else target.at[part],
                send_sem=pass_send.at[j, 4 * dz + dy],
                recv_sem=pass_recv.at[j, 4 * dz + dy],
                device_id={"mode": beside},
                device_id_type=MESH,
            )

        def sent_all(index):
            whole = x[0, 0, 0]
            return pltpu.make_async_remote_copy(
                src_ref=whole,
                dst_ref=whole,
                send_sem=bulk_send.at[j, index],
                recv_sem=bulk_recv.at[j, index, 0],
                device_id={"mode": beside},
                device_id_type=MESH,
            )

        following = {("A1", 0): ("A2", "Z"), ("A1", 2): ("A2", "Z"), ("A3", 1): ("A2", "Z"), ("A3", 3): ("A2", "Z")}
        for q in range(QUARTERS):
            following["Z0", q] = ("B",)
            following["B", q] = ("C2",)

        def take(name, *quarters):
            for q in quarters:
                copy_of(name, q).wait_recv()
                for after in following.get((name, q), ()):
                    copy_of(after, q).start()
                passing(route(name, q)[1], parts[q]).start()

        def send_own(q):
            copy_of("A1", q).start()
            copy_of("A3", q).start()
            copy_of("Z0", q).start()
            passing((0, 0), parts[q]).start()

        sends.extend(sent_all(index) for index in range(len(WIRE)))
        sends.extend(passing(place) for place in PLACES)
        return passing, take, send_own

    gathers = [gather_of(j) for j in range(KRYLOV)]
    for q in range(QUARTERS):
        gathers[0][2](q)

    for j in range(KRYLOV):
        x = held[j]
        now = krylov[j]
        later = krylov[j + 1]

        passing, take, _ = gathers[j]

        def face_block(b, carry):
            low, high = now[b, 0:8, :] * open_ref[0:8, :], now[b, 56:64, :] * open_ref[56:64, :]
            face_out[j, 0, b] = jnp.where(gx == 0, high, low)
            for cell in range(8):
                value = now[b, 8 * cell : 8 * cell + 8, :] * open_ref[8 * cell : 8 * cell + 8, :]
                face_out[j, 1, b, pl.ds(cell, 1), :] = value[7:8, :]
                face_out[j, 2, b, pl.ds(cell, 1), :] = value[0:1, :]
            return carry

        lax.fori_loop(0, local_blocks, face_block, 0)
        faces = [
            pltpu.make_async_remote_copy(
                src_ref=face_out.at[j, side],
                dst_ref=face_in.at[j, side],
                send_sem=face_send.at[j, side],
                recv_sem=face_recv.at[j, side],
                device_id=to,
                device_id_type=MESH,
            )
            for side, to in (
                (0, {"gx": lax.rem(gx + 1, 2)}),
                (1, {"gy": lax.rem(gy + 1, 4)}),
                (2, {"gy": lax.rem(gy + 3, 4)}),
            )
        ]
        start(faces[1])
        start(faces[2])

        def product(place, b):
            owner = mode_of(*place)
            first, second = (
                jnp.clip(col_ref[b, owner * 2 + s] - owner * local_blocks, 0, local_blocks - 1) for s in range(2)
            )
            ref = x[place]
            picked = jnp.concatenate([ref[first], ref[second]], axis=1)
            matrix = weights[8 * place[2] + 4 * place[0] + place[1], b]
            return lax.dot_general(picked, matrix, (((1,), (1,)), ((), ())), preferred_element_type=jnp.float32)

        def ready(place):
            if j == 0:
                for copy in weight_copies(*place):
                    copy.wait()
            if place[2] == 1:
                passing(place[:2]).wait_recv()

        def compute(place):
            ready(place)

            def block(b, carry):
                later[b] = later[b] - product(place, b)
                return carry

            lax.fori_loop(0, local_blocks, block, 0, unroll=True)

        def compute_first(place):
            ready(place)

            def block(b, carry):
                later[b] = -product(place, b)
                return carry

            lax.fori_loop(0, local_blocks, block, 0, unroll=True)

        def local_terms():
            for copy in faces[1:]:
                copy.wait_recv()

            def block(b, carry):
                lanes = lanes_of(b)
                relax = relax_ref[lanes][None, :] - shift
                speed_first, speed_second = drift_ref[0:1, lanes], drift_ref[1:2, lanes]
                to_higher_first = sign_ref[0:1, lanes] == 1
                to_higher_second = sign_ref[1:2, lanes] == 1
                values = [now[b, 8 * cell : 8 * cell + 8, :] for cell in range(8)]
                masked = [values[cell] * open_ref[8 * cell : 8 * cell + 8, :] for cell in range(8)]
                west = [empty] + masked[:7]
                east = masked[1:] + [empty]
                for cell in range(8):
                    rows = slice(8 * cell, 8 * cell + 8)
                    from_low = jnp.where(gy > 0, face_in[j, 1, b, pl.ds(cell, 1), :], 0.0)
                    from_high = jnp.where(gy < 3, face_in[j, 2, b, pl.ds(cell, 1), :], 0.0)
                    south = jnp.where(rows8 == 0, from_low, pltpu.roll(masked[cell], 1, 0))
                    north = jnp.where(rows8 == 7, from_high, pltpu.roll(masked[cell], 7, 0))
                    upstream_first = jnp.where(to_higher_first, west[cell], east[cell])
                    upstream_second = jnp.where(to_higher_second, south, north)
                    value = values[cell]
                    term = speed_first * (value - upstream_first) + speed_second * (value - upstream_second)
                    later[b, rows, :] = later[b, rows, :] + (relax * value + term)
                return carry

            lax.fori_loop(0, local_blocks, block, 0)

        def edge_terms():
            faces[0].wait_recv()
            rows = pl.ds(pl.multiple_of((1 - gx) * 56, 8), 8)

            def block(b, carry):
                lanes = lanes_of(b)
                inward = sign_ref[0:1, lanes] == gx
                later[b, rows, :] = later[b, rows, :] - jnp.where(
                    inward, drift_ref[0:1, lanes] * face_in[j, 0, b], 0.0
                )
                return carry

            lax.fori_loop(0, local_blocks, block, 0)

        def dots_with(k):
            def block(b, carry):
                totals = list(carry)
                for cell in range(8):
                    rows = slice(8 * cell, 8 * cell + 8)
                    value = krylov[k][b, rows, :]
                    for i in range(k + 1):
                        totals[i] = totals[i] + krylov[i][b, rows, :] * value
                return tuple(totals)

            totals = lax.fori_loop(0, local_blocks, block, tuple(empty for i in range(k + 1)))
            for i in range(k + 1):
                grams[i, k] = totals[i]

        compute_first((0, 0, 0))
        compute((0, 0, 1))
        take("A1", 0)
        take("A3", 0)
        take("Z0", 0)
        take("A3", 1)
        take("A1", 1)
        take("Z0", 1)
        dots_with(j)
        if j == 0:
            post(0, 1, collect(0, 0))
        take("A1", 2)
        take("A3", 2)
        take("Z0", 2)
        take("A3", 3)
        take("A1", 3)
        take("Z0", 3)
        start(faces[0])
        compute((0, 1, 0))
        take("B", 0)
        take("A2", 0)
        take("A2", 1)
        compute((0, 3, 0))
        take("B", 1)
        compute((1, 0, 0))
        take("Z", 0)
        compute((0, 1, 1))
        take("B", 2)
        compute((0, 3, 1))
        take("B", 3)
        take("Z", 1)
        take("A2", 2)
        compute((1, 0, 1))
        take("A2", 3)
        if j == 0:
            squared, diagonal = unpack(collect(0, 1), 2)
            shift = diagonal / (squared + epsilon)
        local_terms()
        take("Z", 2)
        compute((0, 2, 0))
        take("C2", 0, 1)
        compute((0, 2, 1))
        take("Z", 3)
        compute((1, 1, 0))
        take("C2", 2)
        compute((1, 3, 0))
        take("C2", 3)
        compute((1, 1, 1))
        compute((1, 3, 1))
        edge_terms()
        compute((1, 2, 0))
        place = (1, 2, 1)
        ready(place)
        if j < KRYLOV - 1:
            nearby = held[j + 1][0, 0, 0]

            for q in range(QUARTERS):
                for b in range(starts[q], ends[q]):
                    value = later[b] - product(place, b)
                    later[b] = value
                    nearby[b] = value.astype(jnp.bfloat16)
                gathers[j + 1][2](q)
        else:

            def final_block(b, carry):
                totals = list(carry)
                value = later[b] - product(place, b)
                for cell in range(8):
                    rows = slice(8 * cell, 8 * cell + 8)
                    part = value[rows, :]
                    for i in range(KRYLOV):
                        totals[i] = totals[i] + krylov[i][b, rows, :] * part
                    totals[KRYLOV] = totals[KRYLOV] + part * part
                return tuple(totals)

            totals = lax.fori_loop(0, local_blocks, final_block, tuple(empty for i in range(KRYLOV + 1)), unroll=True)
            for i in range(KRYLOV + 1):
                grams[i, KRYLOV] = totals[i]

    pairs = [(i, k) for k in range(KRYLOV + 1) for i in range(k + 1)]
    post(1, 0, pack([grams[pair] for pair in pairs]))
    post(1, 1, collect(1, 0))
    sums = dict(zip(pairs, unpack(collect(1, 1), len(pairs))))
    gram = [[sums.get((i, k)) for k in range(KRYLOV + 1)] for i in range(KRYLOV + 1)]
    initial = jnp.sqrt(gram[0][0] + epsilon)
    hessenberg, factors = gram_schmidt(gram, shift, initial)

    def out_block(b, carry):
        lanes = lanes_of(b)
        value = factors[0] * krylov[0][b]
        for k in range(1, KRYLOV):
            value = value + factors[k] * krylov[k][b]
        out_ref[:, :, lanes] = value.reshape(8, 8, LANES)
        return carry

    lax.fori_loop(0, local_blocks, out_block, 0)
    columns = lax.broadcasted_iota(jnp.int32, (8, LANES), 1)
    tile = empty
    for i in range(KRYLOV + 1):
        for k in range(KRYLOV):
            tile = jnp.where((rows8 == i) & (columns == k), hessenberg[i][k], tile)
    hess_ref[...] = tile[: KRYLOV + 1, :KRYLOV]
    for copy in sends:
        copy.wait_send()


def handed_on(solution_in, hessenberg_in, solution_out, hessenberg_out):
    solution_out[...] = solution_in[...]
    hessenberg_out[...] = hessenberg_in[...]


def per_device(right_side, col_block, blocks, relax_rate, drift_speed, upwind_sign, wall_mask):
    cells_first, cells_second, local_modes = right_side.shape
    cells = cells_first * cells_second
    local_blocks = col_block.shape[0]
    block = blocks.shape[2]
    vector = pltpu.VMEM((local_blocks, cells, block), jnp.float32)
    rounded = pltpu.VMEM((local_blocks, cells, block), jnp.bfloat16)
    dma = pltpu.SemaphoreType.DMA
    vmem = pl.BlockSpec(memory_space=pltpu.VMEM)
    solved = pl.pallas_call(
        kernel,
        out_shape=(
            jax.ShapeDtypeStruct(right_side.shape, jnp.float32),
            jax.ShapeDtypeStruct((KRYLOV + 1, KRYLOV), jnp.float32),
        ),
        in_specs=[pl.BlockSpec(memory_space=pl.ANY)] * 7,
        out_specs=(vmem, vmem),
        scratch_shapes=[
            pltpu.SMEM(col_block.shape, jnp.int32),
            pltpu.SMEM(wall_mask.shape, jnp.int32),
            pltpu.VMEM(right_side.shape, jnp.float32),
            pltpu.VMEM(relax_rate.shape, jnp.float32),
            pltpu.VMEM(drift_speed.shape, jnp.float32),
            pltpu.VMEM(upwind_sign.shape, jnp.int32),
            pltpu.VMEM((16, local_blocks, block, 2 * block), jnp.bfloat16),
            pltpu.VMEM((2, 1, LANES), jnp.float32),
            pltpu.VMEM((2, 1, LANES), jnp.float32),
            pltpu.VMEM((2, 8, 1, LANES), jnp.float32),
            pltpu.VMEM((2, 16, 1, LANES), jnp.float32),
            pltpu.VMEM((KRYLOV, 3, local_blocks, 8, LANES), jnp.float32),
            pltpu.VMEM((KRYLOV, 3, local_blocks, 8, LANES), jnp.float32),
            pltpu.VMEM((cells, LANES), jnp.float32),
            dma((6,)),
            dma((16, 2)),
            dma((KRYLOV, len(WIRE))),
            dma((KRYLOV, len(WIRE), QUARTERS)),
            dma((KRYLOV, len(PLACES))),
            dma((KRYLOV, len(PLACES))),
            dma((KRYLOV, 3)),
            dma((KRYLOV, 3)),
            dma((2, 7)),
            dma((2, 7)),
            dma((2, 15)),
            dma((2, 15)),
        ]
        + [vector] * (KRYLOV + 1)
        + [rounded] * (16 * KRYLOV),
        compiler_params=pltpu.CompilerParams(
            collective_id=0, has_side_effects=True, vmem_limit_bytes=60000000
        ),
        name="cycle",
    )(col_block, wall_mask, right_side, relax_rate, drift_speed, upwind_sign, blocks)
    return pl.pallas_call(
        handed_on,
        out_shape=tuple(jax.ShapeDtypeStruct(value.shape, value.dtype) for value in solved),
        in_specs=[vmem, vmem],
        out_specs=(vmem, vmem),
        name="handed_on",
    )(*solved)


def solution(mesh):
    return jax.shard_map(
        per_device,
        mesh=mesh,
        in_specs=(
            P("gx", "gy", "mode"),
            P("mode", None),
            P("mode", None, None, None),
            P("mode"),
            P(None, "mode"),
            P(None, "mode"),
            P("gx", "gy"),
        ),
        out_specs=(P("gx", "gy", "mode"), P()),
        check_vma=False,
    )
```

```python
import functools

import jax
import jax.numpy as jnp
from jax import lax
from jax.experimental import pallas as pl
from jax.experimental.pallas import tpu as pltpu
from jax.sharding import PartitionSpec as P

KRYLOV = 3
MESH = pl.DeviceIdType.MESH
LANES = 128
QUARTERS = 4

epsilon = 1e-12

WIRE = ("A1", "A3", "Z0", "A2", "B", "Z", "C2")
PLACES = [(dz, dy) for dz in range(2) for dy in range(4)]


def least_squares(upper, initial, zero):
    target = [initial] + [zero for row_index in range(KRYLOV)]
    cosines = []
    sines = []
    for col_index in range(KRYLOV):
        for row_index in range(col_index):
            first = upper[row_index][col_index]
            second = upper[row_index + 1][col_index]
            upper[row_index][col_index] = cosines[row_index] * first + sines[row_index] * second
            upper[row_index + 1][col_index] = cosines[row_index] * second - sines[row_index] * first
        first = upper[col_index][col_index]
        second = upper[col_index + 1][col_index]
        radius = jnp.sqrt(first * first + second * second)
        cosine = first / radius
        sine_value = second / radius
        upper[col_index][col_index] = radius
        target[col_index + 1] = -sine_value * target[col_index]
        target[col_index] = cosine * target[col_index]
        cosines.append(cosine)
        sines.append(sine_value)
    combo = [None] * KRYLOV
    for row_index in reversed(range(KRYLOV)):
        running = target[row_index]
        for col_index in range(row_index + 1, KRYLOV):
            running = running - upper[row_index][col_index] * combo[col_index]
        combo[row_index] = running / upper[row_index][row_index]
    return combo


def gram_schmidt(gram, shift, initial):
    size = KRYLOV + 1

    def inner(first, second):
        total = None
        for i in range(size):
            if first[i] is None:
                continue
            row = None
            for k in range(size):
                if second[k] is None:
                    continue
                term = gram[min(i, k)][max(i, k)] * second[k]
                row = term if row is None else row + term
            term = first[i] * row
            total = term if total is None else total + term
        return total

    zero = jnp.zeros_like(initial)
    basis = [[1.0 / initial, None, None, None]]
    hessenberg = [[zero for col in range(KRYLOV)] for row in range(size)]
    for section in range(KRYLOV):
        current = basis[section]
        mapped = [None] * size
        for i in range(size):
            if current[i] is not None:
                own = shift * current[i]
                mapped[i] = own if mapped[i] is None else mapped[i] + own
                mapped[i + 1] = current[i]
        coefficients = [inner(basis[i], mapped) for i in range(section + 1)]
        for i in range(section + 1):
            hessenberg[i][section] = coefficients[i]
            for k in range(size):
                if basis[i][k] is not None:
                    mapped[k] = mapped[k] - coefficients[i] * basis[i][k]
        length = jnp.sqrt(jnp.maximum(inner(mapped, mapped), 0.0) + epsilon)
        hessenberg[section + 1][section] = length
        basis.append([None if value is None else value / length for value in mapped])
    combo = least_squares([list(row) for row in hessenberg], initial, zero)
    weights = []
    for k in range(KRYLOV):
        total = None
        for section in range(KRYLOV):
            if basis[section][k] is not None:
                term = combo[section] * basis[section][k]
                total = term if total is None else total + term
        weights.append(total)
    return hessenberg, weights


def kernel(
    col_hbm,
    wall_hbm,
    right_hbm,
    relax_hbm,
    drift_hbm,
    sign_hbm,
    blocks_ref,
    out_ref,
    hess_ref,
    col_ref,
    wall_ref,
    right_ref,
    relax_ref,
    drift_ref,
    sign_ref,
    weights,
    tile_one,
    tile_two,
    gather_one,
    gather_two,
    face_out,
    face_in,
    open_ref,
    in_sem,
    w_sem,
    bulk_send,
    bulk_recv,
    pass_send,
    pass_recv,
    face_send,
    face_recv,
    one_send,
    one_recv,
    two_send,
    two_recv,
    *slots,
):
    krylov = slots[: KRYLOV + 1]
    held = [
        {(dz, dy, dc): slots[KRYLOV + 1 + 16 * j + 8 * dc + 4 * dz + dy] for dz, dy in PLACES for dc in range(2)}
        for j in range(KRYLOV)
    ]
    local_blocks = col_ref.shape[0]
    ends = [-(-local_blocks * (q + 1) // QUARTERS) for q in range(QUARTERS)]
    starts = [0] + ends[:-1]
    parts = [pl.ds(start, end - start) for start, end in zip(starts, ends)]

    mode = lax.axis_index("mode")
    gx = lax.axis_index("gx")
    gy = lax.axis_index("gy")
    zh = mode // 8
    y = (mode // 2) % 4
    core = mode % 2
    z = zh * 2 + gx

    def mode_of(dz, dy, dc):
        return lax.rem(zh + dz, 2) * 8 + lax.rem(y + dy, 4) * 2 + lax.rem(core + dc, 2)

    def lanes_of(b):
        return pl.ds(pl.multiple_of(b * LANES, LANES), LANES)

    def weight_copies(dz, dy, dc):
        owner = mode_of(dz, dy, dc)
        place = 8 * dc + 4 * dz + dy
        return [
            pltpu.make_async_copy(
                blocks_ref.at[:, owner * 2 + s],
                weights.at[place, :, :, pl.ds(s * LANES, LANES)],
                w_sem.at[place, s],
            )
            for s in range(2)
        ]

    order = [
        (0, 0, 0), (0, 0, 1), (0, 1, 0), (0, 3, 0), (1, 0, 0), (0, 1, 1), (0, 3, 1), (1, 0, 1),
        (0, 2, 0), (0, 2, 1), (1, 1, 0), (1, 3, 0), (1, 1, 1), (1, 3, 1), (1, 2, 0), (1, 2, 1),
    ]
    ring = []
    for d in range(1, 8):
        z_to = lax.rem(z + d // 2, 4)
        ring.append({"mode": z_to // 2 * 8 + y * 2 + lax.rem(core + d % 2, 2), "gx": lax.rem(z_to, 2)})
    plane = [
        {"mode": zh * 8 + lax.rem(y + d // 4, 4) * 2 + core, "gy": lax.rem(gy + d % 4, 4)} for d in range(1, 16)
    ]
    barrier = pltpu.get_barrier_semaphore()
    for partner in plane + ring:
        pl.semaphore_signal(barrier, inc=1, device_id=partner, device_id_type=MESH)

    inputs = [
        pltpu.make_async_copy(source, target, in_sem.at[index])
        for index, (source, target) in enumerate(
            (
                (right_hbm, right_ref),
                (relax_hbm, relax_ref),
                (drift_hbm, drift_ref),
                (sign_hbm, sign_ref),
                (wall_hbm, wall_ref),
                (col_hbm, col_ref),
            )
        )
    ]
    for copy in inputs:
        copy.start()
    for place in order:
        for copy in weight_copies(*place):
            copy.start()
    for copy in inputs:
        copy.wait()

    def norm_block(b, carry):
        plain, weighted = carry
        lanes = lanes_of(b)
        diagonal = relax_ref[lanes][None, :] + drift_ref[0:1, lanes] + drift_ref[1:2, lanes]
        for x in range(8):
            value = right_ref[x, :, lanes]
            square = value * value
            plain = plain + square
            weighted = weighted + square * diagonal
        value = right_ref[:, :, lanes].reshape(64, LANES)
        krylov[0][b] = value
        held[0][0, 0, 0][b] = value.astype(jnp.bfloat16)
        return plain, weighted

    empty = jnp.zeros((8, LANES), jnp.float32)
    plain, weighted = lax.fori_loop(0, local_blocks, norm_block, (empty, empty))
    for x in range(8):
        for cell in range(8):
            open_ref[pl.ds(x * 8 + cell, 1), :] = jnp.full(
                (1, LANES), (1 - wall_ref[x, cell]).astype(jnp.float32), jnp.float32
            )

    pl.semaphore_wait(barrier, 22)

    lane = lax.broadcasted_iota(jnp.int32, (1, LANES), 1)

    stages = (
        (ring, z * 2 + core, 8, tile_one, gather_one, one_send, one_recv),
        (plane, y * 4 + gy, 16, tile_two, gather_two, two_send, two_recv),
    )

    def copies_of(which, stage):
        partners, me, _, tile, places, send, recv = stages[stage]
        return [
            pltpu.make_async_remote_copy(
                src_ref=tile.at[which],
                dst_ref=places.at[which, me],
                send_sem=send.at[which, index],
                recv_sem=recv.at[which, index],
                device_id=partner,
                device_id_type=MESH,
            )
            for index, partner in enumerate(partners)
        ]

    def post(which, stage, value):
        _, me, _, tile, places, _, _ = stages[stage]
        tile[which] = value
        places[which, me] = value
        for copy in copies_of(which, stage):
            copy.start()

    def collect(which, stage):
        _, _, count, _, places, _, _ = stages[stage]
        for copy in copies_of(which, stage):
            copy.wait()
        total = places[which, 0]
        for source in range(1, count):
            total = total + places[which, source]
        return total

    def pack(partials):
        packed = jnp.zeros((1, LANES), jnp.float32)
        for k, partial in enumerate(partials):
            own = jnp.sum(jnp.sum(partial, axis=0, keepdims=True), axis=1, keepdims=True)
            packed = jnp.where(lane == k, own, packed)
        return packed

    def unpack(packed, count):
        return [
            jnp.broadcast_to(jnp.sum(jnp.where(lane == k, packed, 0.0), axis=1, keepdims=True), (1, LANES))
            for k in range(count)
        ]

    post(0, 0, pack([plain, weighted]))
    sends = []
    rows8 = lax.broadcasted_iota(jnp.int32, (8, LANES), 0)
    grams = {}

    def start(copy):
        copy.start()
        sends.append(copy)

    def gather_of(j):
        x = held[j]
        below, above, across, beside = mode_of(0, 3, 0), mode_of(0, 1, 0), mode_of(1, 0, 0), mode_of(0, 0, 1)

        def route(name, q):
            even = q % 2 == 0
            return {
                "A1": ((0, 0), (0, 1), below),
                "A3": ((0, 0), (0, 3), above),
                "Z0": ((0, 0), (1, 0), across),
                "A2": ((0, 1), (0, 2), below) if even else ((0, 3), (0, 2), above),
                "B": ((1, 0), (1, 3), above) if even else ((1, 0), (1, 1), below),
                "Z": ((0, 1), (1, 1), across) if even else ((0, 3), (1, 3), across),
                "C2": ((1, 3), (1, 2), above) if even else ((1, 1), (1, 2), below),
            }[name]

        def copy_of(name, q):
            source, target, to = route(name, q)
            index = WIRE.index(name)
            return pltpu.make_async_remote_copy(
                src_ref=x[source[0], source[1], 0].at[parts[q]],
                dst_ref=x[target[0], target[1], 0].at[parts[q]],
                send_sem=bulk_send.at[j, index],
                recv_sem=bulk_recv.at[j, index, q],
                device_id={"mode": to},
                device_id_type=MESH,
            )

        def passing(place, part=None):
            dz, dy = place
            source, target = x[dz, dy, 0], x[dz, dy, 1]
            return pltpu.make_async_remote_copy(
                src_ref=source if part is None else source.at[part],
                dst_ref=target if part is None else target.at[part],
                send_sem=pass_send.at[j, 4 * dz + dy],
                recv_sem=pass_recv.at[j, 4 * dz + dy],
                device_id={"mode": beside},
                device_id_type=MESH,
            )

        def sent_all(index):
            whole = x[0, 0, 0]
            return pltpu.make_async_remote_copy(
                src_ref=whole,
                dst_ref=whole,
                send_sem=bulk_send.at[j, index],
                recv_sem=bulk_recv.at[j, index, 0],
                device_id={"mode": beside},
                device_id_type=MESH,
            )

        following = {}
        for q in range(QUARTERS):
            following["A3" if q % 2 else "A1", q] = ("A2", "Z")
            following["Z0", q] = ("B",)
            following["B", q] = ("C2",)

        def take(name, *quarters):
            for q in quarters:
                copy_of(name, q).wait_recv()
                for after in following.get((name, q), ()):
                    copy_of(after, q).start()
                passing(route(name, q)[1], parts[q]).start()

        def send_own(q):
            copy_of("A1", q).start()
            copy_of("A3", q).start()
            copy_of("Z0", q).start()
            passing((0, 0), parts[q]).start()

        sends.extend(sent_all(index) for index in range(len(WIRE)))
        sends.extend(passing(place) for place in PLACES)
        return passing, take, send_own

    gathers = [gather_of(j) for j in range(KRYLOV)]
    for q in range(QUARTERS):
        gathers[0][2](q)

    for j in range(KRYLOV):
        x = held[j]
        now = krylov[j]
        later = krylov[j + 1]

        passing, take, _ = gathers[j]

        def face_block(b, carry):
            low, high = now[b, 0:8, :] * open_ref[0:8, :], now[b, 56:64, :] * open_ref[56:64, :]
            face_out[j, 0, b] = jnp.where(gx == 0, high, low)
            for cell in range(8):
                value = now[b, 8 * cell : 8 * cell + 8, :] * open_ref[8 * cell : 8 * cell + 8, :]
                face_out[j, 1, b, pl.ds(cell, 1), :] = value[7:8, :]
                face_out[j, 2, b, pl.ds(cell, 1), :] = value[0:1, :]
            return carry

        lax.fori_loop(0, local_blocks, face_block, 0)
        faces = [
            pltpu.make_async_remote_copy(
                src_ref=face_out.at[j, side],
                dst_ref=face_in.at[j, side],
                send_sem=face_send.at[j, side],
                recv_sem=face_recv.at[j, side],
                device_id=to,
                device_id_type=MESH,
            )
            for side, to in (
                (0, {"gx": lax.rem(gx + 1, 2)}),
                (1, {"gy": lax.rem(gy + 1, 4)}),
                (2, {"gy": lax.rem(gy + 3, 4)}),
            )
        ]
        start(faces[1])
        start(faces[2])

        def product(place, b):
            owner = mode_of(*place)
            first, second = (
                jnp.clip(col_ref[b, owner * 2 + s] - owner * local_blocks, 0, local_blocks - 1) for s in range(2)
            )
            ref = x[place]
            picked = jnp.concatenate([ref[first], ref[second]], axis=1)
            matrix = weights[8 * place[2] + 4 * place[0] + place[1], b]
            return lax.dot_general(picked, matrix, (((1,), (1,)), ((), ())), preferred_element_type=jnp.float32)

        def ready(place):
            if j == 0:
                for copy in weight_copies(*place):
                    copy.wait()
            if place[2] == 1:
                passing(place[:2]).wait_recv()

        def compute(place):
            ready(place)

            def block(b, carry):
                later[b] = later[b] - product(place, b)
                return carry

            lax.fori_loop(0, local_blocks, block, 0, unroll=True)

        def compute_first(place):
            ready(place)

            def block(b, carry):
                later[b] = -product(place, b)
                return carry

            lax.fori_loop(0, local_blocks, block, 0, unroll=True)

        def local_terms():
            for copy in faces[1:]:
                copy.wait_recv()

            def block(b, carry):
                lanes = lanes_of(b)
                relax = relax_ref[lanes][None, :] - shift
                speed_first, speed_second = drift_ref[0:1, lanes], drift_ref[1:2, lanes]
                to_higher_first = sign_ref[0:1, lanes] == 1
                to_higher_second = sign_ref[1:2, lanes] == 1
                values = [now[b, 8 * cell : 8 * cell + 8, :] for cell in range(8)]
                masked = [values[cell] * open_ref[8 * cell : 8 * cell + 8, :] for cell in range(8)]
                west = [empty] + masked[:7]
                east = masked[1:] + [empty]
                for cell in range(8):
                    rows = slice(8 * cell, 8 * cell + 8)
                    from_low = jnp.where(gy > 0, face_in[j, 1, b, pl.ds(cell, 1), :], 0.0)
                    from_high = jnp.where(gy < 3, face_in[j, 2, b, pl.ds(cell, 1), :], 0.0)
                    south = jnp.where(rows8 == 0, from_low, pltpu.roll(masked[cell], 1, 0))
                    north = jnp.where(rows8 == 7, from_high, pltpu.roll(masked[cell], 7, 0))
                    upstream_first = jnp.where(to_higher_first, west[cell], east[cell])
                    upstream_second = jnp.where(to_higher_second, south, north)
                    value = values[cell]
                    term = speed_first * (value - upstream_first) + speed_second * (value - upstream_second)
                    later[b, rows, :] = later[b, rows, :] + (relax * value + term)
                return carry

            lax.fori_loop(0, local_blocks, block, 0)

        def edge_terms():
            faces[0].wait_recv()
            rows = pl.ds(pl.multiple_of((1 - gx) * 56, 8), 8)

            def block(b, carry):
                lanes = lanes_of(b)
                inward = sign_ref[0:1, lanes] == gx
                later[b, rows, :] = later[b, rows, :] - jnp.where(
                    inward, drift_ref[0:1, lanes] * face_in[j, 0, b], 0.0
                )
                return carry

            lax.fori_loop(0, local_blocks, block, 0)

        def dots_with(k):
            def block(b, carry):
                totals = list(carry)
                for cell in range(8):
                    rows = slice(8 * cell, 8 * cell + 8)
                    value = krylov[k][b, rows, :]
                    for i in range(k + 1):
                        totals[i] = totals[i] + krylov[i][b, rows, :] * value
                return tuple(totals)

            totals = lax.fori_loop(0, local_blocks, block, tuple(empty for i in range(k + 1)))
            for i in range(k + 1):
                grams[i, k] = totals[i]

        compute_first((0, 0, 0))
        compute((0, 0, 1))
        dots_with(j)
        take("A1", 0)
        take("A3", 0)
        take("Z0", 0)
        take("A1", 1)
        take("A3", 1)
        if j == 0:
            post(0, 1, collect(0, 0))
        take("Z0", 1)
        take("A1", 2)
        take("A3", 2)
        take("Z0", 2)
        take("A1", 3)
        take("A3", 3)
        start(faces[0])
        compute((0, 1, 0))
        compute((0, 3, 0))
        take("Z0", 3)
        compute((0, 1, 1))
        take("A2", 0)
        take("B", 0)
        compute((0, 3, 1))
        compute((1, 0, 0))
        take("A2", 1)
        take("B", 1)
        take("Z", 0)
        compute((1, 0, 1))
        if j == 0:
            squared, diagonal = unpack(collect(0, 1), 2)
            shift = diagonal / (squared + epsilon)
        local_terms()
        take("Z", 1)
        take("A2", 2)
        take("B", 2)
        take("A2", 3)
        take("B", 3)
        compute((0, 2, 0))
        take("Z", 2)
        compute((1, 1, 0))
        take("C2", 1)
        compute((0, 2, 1))
        take("Z", 3)
        take("C2", 0)
        compute((1, 1, 1))
        compute((1, 3, 0))
        edge_terms()
        compute((1, 3, 1))
        take("C2", 2)
        take("C2", 3)
        compute((1, 2, 0))
        place = (1, 2, 1)
        ready(place)
        if j < KRYLOV - 1:
            nearby = held[j + 1][0, 0, 0]

            for q in range(QUARTERS):
                for b in range(starts[q], ends[q]):
                    value = later[b] - product(place, b)
                    later[b] = value
                    nearby[b] = value.astype(jnp.bfloat16)
                gathers[j + 1][2](q)
        else:

            def final_block(b, carry):
                totals = list(carry)
                value = later[b] - product(place, b)
                for cell in range(8):
                    rows = slice(8 * cell, 8 * cell + 8)
                    part = value[rows, :]
                    for i in range(KRYLOV):
                        totals[i] = totals[i] + krylov[i][b, rows, :] * part
                    totals[KRYLOV] = totals[KRYLOV] + part * part
                return tuple(totals)

            totals = lax.fori_loop(0, local_blocks, final_block, tuple(empty for i in range(KRYLOV + 1)), unroll=True)
            for i in range(KRYLOV + 1):
                grams[i, KRYLOV] = totals[i]

    pairs = [(i, k) for k in range(KRYLOV + 1) for i in range(k + 1)]
    post(1, 0, pack([grams[pair] for pair in pairs]))
    post(1, 1, collect(1, 0))
    sums = dict(zip(pairs, unpack(collect(1, 1), len(pairs))))
    gram = [[sums.get((i, k)) for k in range(KRYLOV + 1)] for i in range(KRYLOV + 1)]
    initial = jnp.sqrt(gram[0][0] + epsilon)
    hessenberg, factors = gram_schmidt(gram, shift, initial)

    def out_block(b, carry):
        lanes = lanes_of(b)
        value = factors[0] * krylov[0][b]
        for k in range(1, KRYLOV):
            value = value + factors[k] * krylov[k][b]
        out_ref[:, :, lanes] = value.reshape(8, 8, LANES)
        return carry

    lax.fori_loop(0, local_blocks, out_block, 0)
    columns = lax.broadcasted_iota(jnp.int32, (8, LANES), 1)
    tile = empty
    for i in range(KRYLOV + 1):
        for k in range(KRYLOV):
            tile = jnp.where((rows8 == i) & (columns == k), hessenberg[i][k], tile)
    hess_ref[...] = tile[: KRYLOV + 1, :KRYLOV]
    for copy in sends:
        copy.wait_send()


def handed_on(solution_in, hessenberg_in, solution_out, hessenberg_out):
    solution_out[...] = solution_in[...]
    hessenberg_out[...] = hessenberg_in[...]


def per_device(right_side, col_block, blocks, relax_rate, drift_speed, upwind_sign, wall_mask):
    cells_first, cells_second, local_modes = right_side.shape
    cells = cells_first * cells_second
    local_blocks = col_block.shape[0]
    block = blocks.shape[2]
    vector = pltpu.VMEM((local_blocks, cells, block), jnp.float32)
    rounded = pltpu.VMEM((local_blocks, cells, block), jnp.bfloat16)
    dma = pltpu.SemaphoreType.DMA
    vmem = pl.BlockSpec(memory_space=pltpu.VMEM)
    solved = pl.pallas_call(
        kernel,
        out_shape=(
            jax.ShapeDtypeStruct(right_side.shape, jnp.float32),
            jax.ShapeDtypeStruct((KRYLOV + 1, KRYLOV), jnp.float32),
        ),
        in_specs=[pl.BlockSpec(memory_space=pl.ANY)] * 7,
        out_specs=(vmem, vmem),
        scratch_shapes=[
            pltpu.SMEM(col_block.shape, jnp.int32),
            pltpu.SMEM(wall_mask.shape, jnp.int32),
            pltpu.VMEM(right_side.shape, jnp.float32),
            pltpu.VMEM(relax_rate.shape, jnp.float32),
            pltpu.VMEM(drift_speed.shape, jnp.float32),
            pltpu.VMEM(upwind_sign.shape, jnp.int32),
            pltpu.VMEM((16, local_blocks, block, 2 * block), jnp.bfloat16),
            pltpu.VMEM((2, 1, LANES), jnp.float32),
            pltpu.VMEM((2, 1, LANES), jnp.float32),
            pltpu.VMEM((2, 8, 1, LANES), jnp.float32),
            pltpu.VMEM((2, 16, 1, LANES), jnp.float32),
            pltpu.VMEM((KRYLOV, 3, local_blocks, 8, LANES), jnp.float32),
            pltpu.VMEM((KRYLOV, 3, local_blocks, 8, LANES), jnp.float32),
            pltpu.VMEM((cells, LANES), jnp.float32),
            dma((6,)),
            dma((16, 2)),
            dma((KRYLOV, len(WIRE))),
            dma((KRYLOV, len(WIRE), QUARTERS)),
            dma((KRYLOV, len(PLACES))),
            dma((KRYLOV, len(PLACES))),
            dma((KRYLOV, 3)),
            dma((KRYLOV, 3)),
            dma((2, 7)),
            dma((2, 7)),
            dma((2, 15)),
            dma((2, 15)),
        ]
        + [vector] * (KRYLOV + 1)
        + [rounded] * (16 * KRYLOV),
        compiler_params=pltpu.CompilerParams(
            collective_id=0, has_side_effects=True, vmem_limit_bytes=60000000
        ),
        name="cycle",
    )(col_block, wall_mask, right_side, relax_rate, drift_speed, upwind_sign, blocks)
    return pl.pallas_call(
        handed_on,
        out_shape=tuple(jax.ShapeDtypeStruct(value.shape, value.dtype) for value in solved),
        in_specs=[vmem, vmem],
        out_specs=(vmem, vmem),
        name="handed_on",
    )(*solved)


def solution(mesh):
    return jax.shard_map(
        per_device,
        mesh=mesh,
        in_specs=(
            P("gx", "gy", "mode"),
            P("mode", None),
            P("mode", None, None, None),
            P("mode"),
            P(None, "mode"),
            P(None, "mode"),
            P("gx", "gy"),
        ),
        out_specs=(P("gx", "gy", "mode"), P()),
        check_vma=False,
    )
```
